32 devices in a mesh: ctx: 8 (over z, y), fsdp: 4 (over x, core).
Axes of the slice: x: 2, y: 2, z: 4, core: 2. Of those that a mesh axis runs over, the one named last changes fastest.
Arguments:
- tokens: bfloat16 [2048, 4096], P('ctx', 'fsdp'), may hold values from -150 to 150
- norm_gain: float32 [4096], replicated, may hold values from 0.1 to 1.9
- in_weight: bfloat16 [4096, 3, 4096], P('ctx', None, 'fsdp'), may hold values from -0.09375 to 0.09375
- short_filter: float32 [3, 3, 4096], P(None, None, 'fsdp'), may hold values from -3.5 to 3.5
- long_filter: bfloat16 [256, 128], P('fsdp'), may hold values from -0.5 to 0.5
- skip_gain: float32 [4096], P('fsdp'), may hold values from -4 to 4
- out_weight: bfloat16 [4096, 4096], P('fsdp', 'ctx'), may hold values from -0.09375 to 0.09375
Outputs:
- mixed: bfloat16 [2048, 4096], P('ctx', 'fsdp')
The draws below stay inside these ranges and needn't reach their ends.
All inputs are finite; a program needn't handle non-finite values.
Results may differ from the reference program's by a relative error of at most 0.0091.
Values may be sent and summed in bfloat16 or wider, within the bound.
A program may use at most 128 MiB of HBM per device.

```python
import math
import jax
import jax.numpy as jnp
from jax import lax

D = 4096
GROUP = 16
GROUPS_WIN = 256
FLEN = 128
CH = 4096
SEQ = 2048


def draw_tokens(key, part):
    first = jax.random.fold_in(key, 11)
    second = jax.random.fold_in(key, 12)
    third = jax.random.fold_in(key, 13)
    base = jnp.clip(jax.random.normal(first, (SEQ, D), jnp.float32), -5.0, 5.0)
    row_scale = jnp.exp(jax.random.uniform(second, (SEQ, 1), jnp.float32, 0.0, math.log(10.0)))
    col_scale = jnp.exp(jax.random.uniform(third, (1, D), jnp.float32, math.log(0.3), math.log(3.0)))
    return (base * row_scale * col_scale).astype(jnp.bfloat16)


def levels(own_key, dims, shards, least, high):
    loudness, own = 1.0, jax.random.fold_in(own_key, 6)
    for dim, parts in shards:
        draws = jnp.exp(jax.random.uniform(jax.random.fold_in(own, dim), (parts,), jnp.float32, least / len(shards), high / len(shards)))
        loudness = loudness * jnp.repeat(draws, dims[dim] // parts).reshape([-1 if axis == dim else 1 for axis in range(len(dims))])
    return loudness


def gaussian(stream_key, dims, width, reach, cuts=(), held_as=jnp.bfloat16):
    values = width * jax.random.normal(stream_key, dims, jnp.float32)
    if cuts:
        values = values * levels(stream_key, dims, cuts, -0.22, 0.18)
    return jnp.clip(values, -reach, reach).astype(held_as)


def setup_inputs(seed: int = 0) -> dict:
    key_of = jax.random.split(jax.random.key(seed), 8)
    tokens = draw_tokens(jax.random.fold_in(key_of[7], 71), 0)
    norm_gain = jnp.clip(1.0 + 0.18 * jax.random.normal(key_of[1], (D,), jnp.float32), 0.1, 1.9)
    in_weight = gaussian(key_of[2], (D, 3, CH), D ** -0.5, 0.09375, ((0, 8), (2, 4)))
    short_filter = gaussian(key_of[3], (3, 3, CH), 3 ** -0.5, 3.5, ((2, 4),), jnp.float32)
    long_filter = gaussian(key_of[4], (GROUPS_WIN, FLEN), FLEN ** -0.5, 0.5, ((0, 4),))
    skip_gain = gaussian(key_of[5], (CH,), 1.0, 4.0, ((0, 4),), jnp.float32)
    out_weight = gaussian(key_of[6], (CH, D), CH ** -0.5, 0.09375, ((0, 4), (1, 8)))
    return {"tokens": tokens, "norm_gain": norm_gain, "in_weight": in_weight, "short_filter": short_filter, "long_filter": long_filter, "skip_gain": skip_gain, "out_weight": out_weight}


def reference(tokens, norm_gain, in_weight, short_filter, long_filter, skip_gain, out_weight):
    filters = jnp.repeat(long_filter, GROUP, axis=0).astype(jnp.float32)
    values = tokens.astype(jnp.float32)
    mean_square = lax.optimization_barrier(jnp.mean(values * values, axis=-1, keepdims=True))
    normed = (values * lax.rsqrt(mean_square + 1e-06) * norm_gain).astype(jnp.bfloat16)
    proj = jnp.dot(normed, in_weight.reshape(D, 3 * CH), preferred_element_type=jnp.float32).astype(jnp.bfloat16)
    projf = proj.astype(jnp.float32).reshape(SEQ, 3, CH)
    padded = jnp.pad(projf, ((2, 0), (0, 0), (0, 0)))
    filtered = short_filter[0] * projf + short_filter[1] * padded[1:-1] + short_filter[2] * padded[:-2]
    out_gate = filtered[:, 0]
    key_part = filtered[:, 1]
    value_part = filtered[:, 2]
    product = (key_part * value_part).astype(jnp.bfloat16)
    prodf = product.astype(jnp.float32)
    extended = jnp.concatenate([jnp.zeros((FLEN - 1, CH), jnp.float32), prodf], axis=0)

    def add_tap(tap_index, accum):
        shifted = lax.dynamic_slice_in_dim(extended, (FLEN - 1 - tap_index).astype(jnp.int32), SEQ, 0)
        return accum + filters[:, tap_index] * shifted
    conv = lax.fori_loop(0, FLEN, add_tap, jnp.zeros((SEQ, CH), jnp.float32))
    gated = (out_gate * (conv + skip_gain * prodf)).astype(jnp.bfloat16)
    return jnp.dot(gated, out_weight, preferred_element_type=jnp.float32).astype(jnp.bfloat16)
```

```python
import functools

import jax
import jax.numpy as jnp
from jax import lax
from jax.experimental import pallas as pl
from jax.experimental.pallas import tpu as pltpu
from jax.sharding import PartitionSpec as P


def passed_along(block, axis, distance):
    devices = range(lax.axis_size(axis))
    route = [(i - distance, i) for i in devices if i - distance in devices]
    return lax.ppermute(block, axis, route)


def toeplitz_blocks(long_filter, row_count):
    groups = long_filter.shape[0]
    flen = long_filter.shape[1]
    window = flen + row_count - 1
    reversed_taps = long_filter[:, ::-1]
    padded = jnp.concatenate(
        [reversed_taps, jnp.zeros((groups, row_count), long_filter.dtype)], axis=1
    )
    tiled = jnp.tile(padded, (1, row_count))
    return tiled[:, : row_count * window].reshape(groups, row_count, window)


def short_conv(taps, extended):
    return taps[0] * extended[2:] + taps[1] * extended[1:-1] + taps[2] * extended[:-2]


def slab_plan(tokens, norm_gain, in_weight, short_filter, long_filter, skip_gain, out_weight):
    whole = lax.all_gather(tokens, "fsdp", axis=1, tiled=True)
    row_count = whole.shape[0]
    values = whole.astype(jnp.float32)
    mean_square = jnp.mean(values * values, axis=-1, keepdims=True)
    normed = (values * lax.rsqrt(mean_square + 1e-06) * norm_gain).astype(jnp.bfloat16)
    share = in_weight.shape[2]
    width_all = 3 * share
    weight_rows = lax.all_gather(in_weight, "ctx", axis=0, tiled=True)
    flat_rows = weight_rows.reshape(weight_rows.shape[0], width_all)
    proj = jnp.dot(normed, flat_rows, preferred_element_type=jnp.float32).astype(jnp.bfloat16)
    taps = short_filter.reshape(3, width_all)
    flen = long_filter.shape[1]
    earlier = passed_along(proj[row_count - 2 :], "ctx", 1)
    extended = jnp.concatenate([earlier, proj], axis=0).astype(jnp.float32)
    filtered = short_conv(taps, extended)
    out_gate = filtered[:, :share]
    product = (filtered[:, share : 2 * share] * filtered[:, 2 * share :]).astype(jnp.bfloat16)
    previous = passed_along(product[row_count - (flen - 1) :], "ctx", 1)
    product_ext = jnp.concatenate([previous, product], axis=0)
    groups = long_filter.shape[0]
    group_width = share // groups
    window = row_count + flen - 1
    blocks = toeplitz_blocks(long_filter, row_count)
    conv = jnp.einsum(
        "gts,sgc->tgc",
        blocks,
        product_ext.reshape(window, groups, group_width),
        preferred_element_type=jnp.float32,
    ).reshape(row_count, share)
    gated = (out_gate * (conv + skip_gain * product.astype(jnp.float32))).astype(jnp.bfloat16)
    terms = jnp.dot(
        gated,
        lax.all_gather(out_weight, "ctx", axis=1, tiled=True),
        preferred_element_type=jnp.float32,
    )
    mixed = lax.psum_scatter(terms, "fsdp", scatter_dimension=1, tiled=True).astype(jnp.bfloat16)
    return mixed


MESH = pl.DeviceIdType.MESH
LANE = 128
TILE = 256


def visit_when(condition, action):
    @pl.when(condition)
    def _():
        action()


def block_kernel(
    group_width, tokens_ref, gain_ref, weight_ref, taps_ref, filter_ref, skip_ref, out_weight_ref,
    out_ref,
    x_all, w_all, acc, sums, bands, halo_out, halo_in, gated, gated_other, o_all,
    terms, kept, cross_out, cross_in, ready,
    x_send, x_recv, s_send, s_recv, w_local, w_send, y_send, w_recv, h_send, h_recv,
    g_send, g_recv, c_send, c_recv, o_local, o_send, o_recv, t_send, t_recv,
    f_local, f_send, f_recv,
):
    ctx, fsdp = lax.axis_index("ctx"), lax.axis_index("fsdp")
    line, parts = lax.axis_size("ctx") // 2, lax.axis_size("fsdp")
    z, y, x, core = ctx // 2, ctx % 2, fsdp // 2, fsdp % 2
    rows, features = tokens_ref.shape
    kinds, depth, share = weight_ref.shape
    own = share // line
    flen = filter_ref.shape[1]
    groups = own // group_width
    fold = LANE // group_width
    half, quarter = rows // 2, rows // 4
    last = line - 1

    here = (ctx, fsdp)
    beside_y = (z * 2 + 1 - y, fsdp)
    beside_x = (ctx, (1 - x) * 2 + core)
    beside_core = (ctx, x * 2 + 1 - core)

    def level(at):
        return (at * 2 + y, fsdp)

    def remote(source, target, sent, received, device):
        return pltpu.make_async_remote_copy(
            src_ref=source, dst_ref=target, send_sem=sent, recv_sem=received,
            device_id=device, device_id_type=MESH,
        )

    peers = [
        ((z + dz) % line * 2 + y, (fsdp + df) % parts)
        for dz in range(line) for df in range(parts) if dz or df
    ]
    barrier = pltpu.get_barrier_semaphore()
    for peer in peers + [beside_y]:
        pl.semaphore_signal(barrier, inc=1, device_id=peer, device_id_type=MESH)

    values = tokens_ref[...].astype(jnp.float32)
    scaled = (values * gain_ref[pl.ds(fsdp, 1), :]).astype(jnp.bfloat16)
    for side in range(2):
        x_all[2 * fsdp + side, pl.ds(pl.multiple_of(z * rows, rows), rows), :] = (
            scaled[:, side * depth : (side + 1) * depth]
        )
    squares = values * values
    coarse = squares.astype(jnp.bfloat16)
    fine = (squares - coarse.astype(jnp.float32)).astype(jnp.bfloat16)
    ones = jnp.ones((8, features), jnp.bfloat16)
    contract = (((1,), (1,)), ((), ()))
    total = lax.dot_general(ones, coarse, contract, preferred_element_type=jnp.float32)
    total += lax.dot_general(ones, fine, contract, preferred_element_type=jnp.float32)
    sums[fsdp * line + z] = total
    pl.semaphore_wait(barrier, len(peers) + 1)

    def x_place(part, at):
        return x_all.at[pl.ds(2 * part, 2), pl.ds(pl.multiple_of(at * rows, rows), rows), :]

    x_targets = [((z + 1) * 2 + y, fsdp), ((z - 1) * 2 + y, fsdp), beside_x, beside_core]
    part_x = (1 - x) * 2 + core

    def x_copy(kind, part, at):
        block = part * line + at
        place = x_place(part, at)
        return remote(place, place, x_send.at[kind, block], x_recv.at[block], x_targets[kind])

    def x_arrive(part, at):
        place = x_place(part, at)
        block = part * line + at
        remote(place, place, x_send.at[0, block], x_recv.at[block], here).wait_recv()

    def x_pass(at, up, down):
        if up:
            visit_when(z < last, lambda: x_copy(0, fsdp, at).start())
        if down:
            visit_when(z > 0, lambda: x_copy(1, fsdp, at).start())
        x_copy(2, fsdp, at).start()
        x_copy(3, fsdp, at).start()

    def x_step(away):
        @pl.when(z >= away)
        def _():
            x_arrive(fsdp, z - away)
            x_pass(z - away, True, False)

        @pl.when(z + away <= last)
        def _():
            x_arrive(fsdp, z + away)
            x_pass(z + away, False, True)

    def x_over(away):
        def take(at):
            x_arrive(part_x, at)
            x_copy(3, part_x, at).start()

        if away == 0:
            take(z)
        else:
            visit_when(z >= away, lambda: take(z - away))
            visit_when(z + away <= last, lambda: take(z + away))

    def piece(kind, at):
        return weight_ref.at[kind, :, pl.ds(pl.multiple_of(at * own, own), own)]

    def landing(kind, at, side):
        return w_all.at[2 * at + side, kind]

    def w_copy(kind, to):
        return remote(
            piece(kind, to), landing(kind, z, y),
            w_send.at[to, kind], w_recv.at[2 * z + y, kind], level(to),
        )

    def w_over(kind, at, mine):
        source = piece(kind, z) if mine else landing(kind, at, y)
        return remote(
            source, landing(kind, at, y),
            y_send.at[at, kind], w_recv.at[2 * at + y, kind], beside_y,
        )

    def w_arrive(kind, at, side):
        place = landing(kind, at, side)
        remote(place, place, y_send.at[at, kind], w_recv.at[2 * at + side, kind], here).wait_recv()

    others = [z + 1 - 2 * (z % 2), (z + 2) % line, last - z]

    def w_spread(step):
        for kind in range(kinds):
            w_copy(kind, others[step]).start()

    def w_turn(step):
        for kind in range(kinds):
            w_arrive(kind, others[step], y)
            w_over(kind, others[step], False).start()

    def multiply(at, side, kind_list, first=False):
        index = 2 * at + side

        def body(step, carry):
            span = pl.ds(pl.multiple_of(step * TILE, TILE), TILE)
            left = x_all[index, span, :]
            for kind in kind_list:
                part = jnp.dot(left, w_all[index, kind], preferred_element_type=jnp.float32)
                if first:
                    acc[kind, span, :] = part
                else:
                    acc[kind, span, :] += part
            return carry

        lax.fori_loop(0, rows * line // TILE, body, 0)

    def s_copy(index):
        place = sums.at[fsdp * line + z]
        return remote(place, place, s_send.at[index], s_recv.at[fsdp * line + z], peers[index])

    def o_copy(index):
        place = o_all.at[core, 1 - y] if index == 2 else o_all.at[core, y]
        source = o_all.at[core, 1 - y] if index == 2 else out_weight_ref
        device = beside_y if index == 0 else beside_core
        return remote(source, place, o_send.at[index], o_recv.at[index], device)

    def o_arrive(index):
        place = (o_all.at[core, 1 - y], o_all.at[1 - core, y], o_all.at[1 - core, 1 - y])[index]
        remote(place, place, o_send.at[index], o_recv.at[index], here).wait_recv()

    w_own = [
        pltpu.make_async_copy(piece(kind, z), landing(kind, z, y), w_local.at[kind])
        for kind in range(kinds)
    ]
    o_own = pltpu.make_async_copy(out_weight_ref, o_all.at[core, y], o_local.at[0])

    x_pass(z, True, True)
    for kind in range(kinds):
        w_over(kind, z, True).start()
    w_spread(0)
    for index in range(len(peers)):
        s_copy(index).start()
    for copy in w_own:
        copy.start()
    o_own.start()
    o_copy(1).start()

    flip = (
        lax.broadcasted_iota(jnp.int32, (flen, flen), 0)
        + lax.broadcasted_iota(jnp.int32, (flen, flen), 1)
    ) == flen - 1
    filters = filter_ref[pl.ds(pl.multiple_of(z * groups, groups), groups), :]
    turned = jnp.dot(filters, flip.astype(jnp.bfloat16), preferred_element_type=jnp.float32)
    base = jnp.concatenate([turned, jnp.zeros_like(turned)], axis=1)
    base = pltpu.roll(base, 1, 1)
    for group in range(groups):
        row = jnp.broadcast_to(base[group : group + 1, :], (flen, 2 * flen))
        band = pltpu.roll(row, 0, 1, stride=1, stride_axis=0)
        bands[pl.ds(group * flen, flen), :] = band.astype(jnp.bfloat16)
    halo_in[0] = jnp.zeros(halo_in.shape[1:], halo_in.dtype)

    x_step(1)
    w_spread(1)
    x_over(0)
    x_step(2)
    w_spread(2)
    x_over(1)
    x_step(3)
    x_over(2)
    w_turn(0)
    x_over(3)
    for part in (x * 2 + 1 - core, (1 - x) * 2 + 1 - core):
        for at in range(line):
            x_arrive(part, at)
    every = range(kinds)
    for copy in w_own:
        copy.wait()
    multiply(z, y, every, True)
    for kind in every:
        w_arrive(kind, z, 1 - y)
    multiply(z, 1 - y, every)
    multiply(others[0], y, every)
    w_turn(1)
    for kind in every:
        w_arrive(kind, others[0], 1 - y)
    multiply(others[0], 1 - y, every)
    multiply(others[1], y, every)
    w_turn(2)
    o_copy(0).start()
    for kind in every:
        w_arrive(kind, others[1], 1 - y)
    multiply(others[1], 1 - y, every)
    multiply(others[2], y, every)
    for index in range(len(peers)):
        peer = peers[index]
        block = peer[1] * line + peer[0] // 2
        place = sums.at[block]
        remote(place, place, s_send.at[index], s_recv.at[block], here).wait_recv()
    for kind in every:
        w_arrive(kind, others[2], 1 - y)
        multiply(others[2], 1 - y, (kind,))

    taps = taps_ref[:, :, pl.ds(pl.multiple_of(z * own, own), own)]
    skip = skip_ref[:, pl.ds(pl.multiple_of(z * own, own), own)]

    def h_copy(slab):
        return remote(
            halo_out.at[slab], halo_in.at[slab + 1],
            h_send.at[slab], h_recv.at[slab + 1], beside_y,
        )

    def h_arrive(slot):
        place = halo_in.at[slot]
        remote(place, place, h_send.at[0], h_recv.at[slot], here).wait_recv()

    def tap(index, kind):
        return taps[index, kind : kind + 1, :]

    for slab in range(line):
        square = sums[slab]
        for part in range(1, parts):
            square = square + sums[part * line + slab]
        mean = square[:1] / (features * parts)
        scale = jnp.broadcast_to(lax.rsqrt(mean + 1e-06), (LANE, rows)).T
        scale = jnp.concatenate([scale] * (own // LANE), axis=1)
        start = slab * rows
        for kind in every:
            exact = (acc[kind, start : start + rows, :] * scale).astype(jnp.bfloat16)
            acc[kind, start : start + rows, :] = exact.astype(jnp.float32)
            halo_out[slab, kind * 16 : (kind + 1) * 16, :] = exact[rows - 16 :]
        tails = []
        for kind in (1, 2):
            end = start + rows
            tails.append(
                tap(0, kind) * acc[kind, end - flen : end, :]
                + tap(1, kind) * acc[kind, end - flen - 1 : end - 1, :]
                + tap(2, kind) * acc[kind, end - flen - 2 : end - 2, :]
            )
        halo_out[slab, kinds * 16 :, :] = (tails[0] * tails[1]).astype(jnp.bfloat16)
        h_copy(slab).start()

    lane_group = lax.broadcasted_iota(jnp.int32, (flen, LANE), 1) // group_width

    def mix(slab):
        if slab > 0:
            visit_when(y == 0, lambda: h_arrive(slab))
        visit_when(y == 1, lambda: h_arrive(slab + 1))
        start = slab * rows
        filtered = []
        for kind in every:
            ahead = halo_in[slab + y, kind * 16 : (kind + 1) * 16, :].astype(jnp.float32)
            extended = jnp.concatenate([ahead[8:], acc[kind, start : start + rows, :]], axis=0)
            filtered.append(short_conv([tap(index, kind) for index in range(3)], extended[6:]))
        gate, key_part, value_part = filtered
        product = (key_part * value_part).astype(jnp.bfloat16)
        reach = jnp.concatenate([halo_in[slab + y, kinds * 16 :, :], product], axis=0)
        for strip in range(own // LANE):
            lanes = slice(strip * LANE, (strip + 1) * LANE)
            matrix = bands[strip * fold * flen : (strip + 1) * fold * flen, :]
            for at in range(0, rows, flen):
                spread = jnp.dot(
                    matrix, reach[at : at + 2 * flen, lanes], preferred_element_type=jnp.float32
                )
                conv = spread[:flen]
                for group in range(1, fold):
                    conv = jnp.where(
                        lane_group == group, spread[group * flen : (group + 1) * flen], conv
                    )
                result = gate[at : at + flen, lanes] * (
                    conv + skip[:, lanes] * product[at : at + flen, lanes].astype(jnp.float32)
                )
                gated[
                    start + at : start + at + flen,
                    pl.ds(pl.multiple_of(z * own + strip * LANE, LANE), LANE),
                ] = result.astype(jnp.bfloat16)

    def g_place(slab, at):
        return gated.at[pl.ds(slab * rows, rows), pl.ds(pl.multiple_of(at * own, own), own)]

    def g_copy(kind, slab, at):
        place = g_place(slab, at)
        return remote(
            place, place, g_send.at[kind, slab, at], g_recv.at[slab, at], x_targets[kind]
        )

    def g_arrive(slab, at):
        place = g_place(slab, at)
        remote(place, place, g_send.at[0, slab, at], g_recv.at[slab, at], here).wait_recv()

    def g_step(slab, away):
        if away == 0:
            visit_when(z < last, lambda: g_copy(0, slab, z).start())
            visit_when(z > 0, lambda: g_copy(1, slab, z).start())
            return

        @pl.when(z >= away)
        def _():
            g_arrive(slab, z - away)
            visit_when(z < last, lambda: g_copy(0, slab, z - away).start())

        @pl.when(z + away <= last)
        def _():
            g_arrive(slab, z + away)
            visit_when(z > 0, lambda: g_copy(1, slab, z + away).start())

    def c_copy(slab):
        return remote(
            gated.at[pl.ds(pl.multiple_of(slab * rows + (1 - core) * half, half), half), :],
            gated_other.at[pl.ds(slab * half, half), :],
            c_send.at[slab], c_recv.at[slab], beside_core,
        )

    def t_copy(slab):
        return remote(
            cross_out.at[slab], cross_in.at[slab], t_send.at[slab], t_recv.at[slab], beside_x
        )

    def project(slab):
        c_copy(slab).wait_recv()
        mine = gated[pl.ds(pl.multiple_of(slab * rows + core * half, half), half), :]
        other = gated_other[pl.ds(slab * half, half), :]
        for side in range(2):
            part = jnp.dot(mine, o_all[core, side], preferred_element_type=jnp.float32)
            part += jnp.dot(other, o_all[1 - core, side], preferred_element_type=jnp.float32)
            width = part.shape[1]
            terms[:, side * width : (side + 1) * width] = part
        kept[slab] = terms[pl.ds(pl.multiple_of(x * quarter, quarter), quarter), :]
        cross_out[slab] = terms[
            pl.ds(pl.multiple_of((1 - x) * quarter, quarter), quarter), :
        ].astype(jnp.bfloat16)
        t_copy(slab).start()

    def out_place(x_from, core_from):
        start = pl.multiple_of(core_from * half + x_from * quarter, quarter)
        return out_ref.at[pl.ds(start, quarter), :]

    lands = fsdp == z

    def f_copy(slab):
        return remote(
            ready.at[slab], out_place(x, core), f_send.at[slab], f_recv.at[fsdp],
            (slab * 2 + y, z),
        )

    def f_stay(slab):
        return pltpu.make_async_copy(ready.at[slab], out_place(x, core), f_local.at[0])

    def hand_over(slab):
        t_copy(slab).wait_recv()
        ready[slab] = (kept[slab] + cross_in[slab].astype(jnp.float32)).astype(jnp.bfloat16)
        stays = lands & (z == slab)
        visit_when(stays, lambda: f_stay(slab).start())
        visit_when(jnp.logical_not(stays), lambda: f_copy(slab).start())

    for turn in range(line + 5):
        if turn < line:
            mix(turn)
            g_step(turn, 0)
        for away in range(1, line):
            if 0 <= turn - away < line:
                g_step(turn - away, away)
        if 0 <= turn - last < line:
            c_copy(turn - last).start()
        if turn == line - 1:
            o_arrive(0)
            o_copy(2).start()
            o_own.wait()
            o_arrive(1)
            o_arrive(2)
        if 0 <= turn - last - 1 < line:
            project(turn - last - 1)
        if 0 <= turn - last - 2 < line:
            hand_over(turn - last - 2)

    for source in range(parts):
        place = out_place(source // 2, source % 2)

        @pl.when(jnp.logical_not(lands & (fsdp == source)))
        def _():
            remote(ready.at[0], place, f_send.at[0], f_recv.at[source], here).wait_recv()

    for at in range(line):
        visit_when((z >= at) & (z < last), lambda: x_copy(0, fsdp, at).wait_send())
        visit_when((z <= at) & (z > 0), lambda: x_copy(1, fsdp, at).wait_send())
        x_copy(2, fsdp, at).wait_send()
        x_copy(3, fsdp, at).wait_send()
        x_copy(3, part_x, at).wait_send()
        for kind in every:
            w_over(kind, at, False).wait_send()
    for index in range(len(peers)):
        s_copy(index).wait_send()
    for kind in every:
        for step in range(3):
            w_copy(kind, others[step]).wait_send()
    visit_when(y == 0, lambda: h_arrive(line))
    for index in range(3):
        o_copy(index).wait_send()
    for slab in range(line):
        h_copy(slab).wait_send()
        c_copy(slab).wait_send()
        t_copy(slab).wait_send()
        for at in range(line):
            visit_when((z >= at) & (z < last), lambda: g_copy(0, slab, at).wait_send())
            visit_when((z <= at) & (z > 0), lambda: g_copy(1, slab, at).wait_send())
        stays = lands & (z == slab)
        visit_when(stays, lambda: f_stay(slab).wait())
        visit_when(jnp.logical_not(stays), lambda: f_copy(slab).wait_send())


VMEM_SPEC = pl.BlockSpec(memory_space=pltpu.VMEM)
ANY_SPEC = pl.BlockSpec(memory_space=pl.ANY)
DMA = pltpu.SemaphoreType.DMA


def level_plan(tokens, norm_gain, in_weight, short_filter, long_filter, skip_gain, out_weight):
    slabs, parts = lax.axis_size("ctx"), lax.axis_size("fsdp")
    line = slabs // 2
    rows, features = tokens.shape
    depth, kinds, share = in_weight.shape
    own = share // line
    flen = long_filter.shape[1]
    group_width = share // long_filter.shape[0]
    groups = own // group_width
    positions = rows * line
    columns = out_weight.shape[1]
    low, full = jnp.bfloat16, jnp.float32
    half, quarter = rows // 2, rows // 4
    return pl.pallas_call(
        functools.partial(block_kernel, group_width),
        out_shape=jax.ShapeDtypeStruct(tokens.shape, low),
        in_specs=[VMEM_SPEC, VMEM_SPEC, ANY_SPEC, VMEM_SPEC, VMEM_SPEC, VMEM_SPEC, ANY_SPEC],
        out_specs=ANY_SPEC,
        scratch_shapes=[
            pltpu.VMEM((2 * parts, positions, depth), low),
            pltpu.VMEM((slabs, kinds, depth, own), low),
            pltpu.VMEM((kinds, positions, own), full),
            pltpu.VMEM((parts * line, 8, rows), full),
            pltpu.VMEM((groups * flen, 2 * flen), low),
            pltpu.VMEM((line, kinds * 16 + flen, own), low),
            pltpu.VMEM((line + 1, kinds * 16 + flen, own), low),
            pltpu.VMEM((positions, share), low),
            pltpu.VMEM((positions // 2, share), low),
            pltpu.VMEM((2, 2, share, columns), low),
            pltpu.VMEM((half, 2 * columns), full),
            pltpu.VMEM((line, quarter, 2 * columns), full),
            pltpu.VMEM((line, quarter, 2 * columns), low),
            pltpu.VMEM((line, quarter, 2 * columns), low),
            pltpu.VMEM((line, quarter, 2 * columns), low),
            DMA((4, parts * line)), DMA((parts * line,)),
            DMA((parts * line,)), DMA((parts * line,)),
            DMA((kinds,)), DMA((line, kinds)), DMA((line, kinds)), DMA((slabs, kinds)),
            DMA((line,)), DMA((line + 1,)),
            DMA((2, line, line)), DMA((line, line)),
            DMA((line,)), DMA((line,)),
            DMA((1,)), DMA((3,)), DMA((3,)),
            DMA((line,)), DMA((line,)),
            DMA((1,)), DMA((line,)), DMA((parts,)),
        ],
        compiler_params=pltpu.CompilerParams(
            collective_id=0, has_side_effects=True, vmem_limit_bytes=48 * 2**20
        ),
    )(
        tokens, norm_gain.reshape(parts, features), in_weight.transpose(1, 0, 2), short_filter,
        long_filter, skip_gain[None], out_weight,
    )


def on_device(tokens, *rest):
    slabs, parts = lax.axis_size("ctx"), lax.axis_size("fsdp")
    depth, _, share = rest[1].shape
    groups, flen = rest[3].shape
    own = share // (slabs // 2)
    fits = (
        parts == 4 and slabs == 8 and tokens.shape[0] == 2 * flen and flen == LANE
        and tokens.shape[1] == 2 * depth and own % LANE == 0 and share == tokens.shape[1]
        and LANE % (share // groups) == 0 and depth * share <= 2**19
    )
    return (level_plan if fits else slab_plan)(tokens, *rest)


def solution(mesh):
    in_specs = (
        P("ctx", "fsdp"),
        P(),
        P("ctx", None, "fsdp"),
        P(None, None, "fsdp"),
        P("fsdp", None),
        P("fsdp"),
        P("fsdp", "ctx"),
    )
    out_specs = P("ctx", "fsdp")
    return jax.shard_map(
        on_device, mesh=mesh, in_specs=in_specs, out_specs=out_specs, check_vma=False
    )
```

```python
import functools

import jax
import jax.numpy as jnp
from jax import lax
from jax.experimental import pallas as pl
from jax.experimental.pallas import tpu as pltpu
from jax.sharding import PartitionSpec as P


def passed_along(block, axis, distance):
    devices = range(lax.axis_size(axis))
    route = [(i - distance, i) for i in devices if i - distance in devices]
    return lax.ppermute(block, axis, route)


def toeplitz_blocks(long_filter, row_count):
    groups = long_filter.shape[0]
    flen = long_filter.shape[1]
    window = flen + row_count - 1
    reversed_taps = long_filter[:, ::-1]
    padded = jnp.concatenate(
        [reversed_taps, jnp.zeros((groups, row_count), long_filter.dtype)], axis=1
    )
    tiled = jnp.tile(padded, (1, row_count))
    return tiled[:, : row_count * window].reshape(groups, row_count, window)


def short_conv(taps, extended):
    return taps[0] * extended[2:] + taps[1] * extended[1:-1] + taps[2] * extended[:-2]


def slab_plan(tokens, norm_gain, in_weight, short_filter, long_filter, skip_gain, out_weight):
    whole = lax.all_gather(tokens, "fsdp", axis=1, tiled=True)
    row_count = whole.shape[0]
    values = whole.astype(jnp.float32)
    mean_square = jnp.mean(values * values, axis=-1, keepdims=True)
    normed = (values * lax.rsqrt(mean_square + 1e-06) * norm_gain).astype(jnp.bfloat16)
    share = in_weight.shape[2]
    width_all = 3 * share
    weight_rows = lax.all_gather(in_weight, "ctx", axis=0, tiled=True)
    flat_rows = weight_rows.reshape(weight_rows.shape[0], width_all)
    proj = jnp.dot(normed, flat_rows, preferred_element_type=jnp.float32).astype(jnp.bfloat16)
    taps = short_filter.reshape(3, width_all)
    flen = long_filter.shape[1]
    earlier = passed_along(proj[row_count - 2 :], "ctx", 1)
    extended = jnp.concatenate([earlier, proj], axis=0).astype(jnp.float32)
    filtered = short_conv(taps, extended)
    out_gate = filtered[:, :share]
    product = (filtered[:, share : 2 * share] * filtered[:, 2 * share :]).astype(jnp.bfloat16)
    previous = passed_along(product[row_count - (flen - 1) :], "ctx", 1)
    product_ext = jnp.concatenate([previous, product], axis=0)
    groups = long_filter.shape[0]
    group_width = share // groups
    window = row_count + flen - 1
    blocks = toeplitz_blocks(long_filter, row_count)
    conv = jnp.einsum(
        "gts,sgc->tgc",
        blocks,
        product_ext.reshape(window, groups, group_width),
        preferred_element_type=jnp.float32,
    ).reshape(row_count, share)
    gated = (out_gate * (conv + skip_gain * product.astype(jnp.float32))).astype(jnp.bfloat16)
    terms = jnp.dot(
        gated,
        lax.all_gather(out_weight, "ctx", axis=1, tiled=True),
        preferred_element_type=jnp.float32,
    )
    mixed = lax.psum_scatter(terms, "fsdp", scatter_dimension=1, tiled=True).astype(jnp.bfloat16)
    return mixed


MESH = pl.DeviceIdType.MESH
LANE = 128
TILE = 256


def visit_when(condition, action):
    @pl.when(condition)
    def _():
        action()


def block_kernel(
    group_width, tokens_hbm, gain_hbm, weight_ref, taps_hbm, filter_hbm, skip_hbm, out_weight_ref,
    out_ref,
    tokens_ref, gain_ref, taps_ref, filter_ref, skip_ref, x_all, w_all, acc, sums, bands, halo_out, halo_in, gated, gated_other, o_all,
    terms, kept, cross_out, cross_in, ready,
    inputs, x_send, x_recv, s_send, s_recv, w_local, w_send, y_send, w_recv, h_send, h_recv,
    g_send, g_recv, c_send, c_recv, o_local, o_send, o_recv, t_send, t_recv,
    f_local, f_send, f_recv,
):
    ctx, fsdp = lax.axis_index("ctx"), lax.axis_index("fsdp")
    line, parts = lax.axis_size("ctx") // 2, lax.axis_size("fsdp")
    z, y, x, core = ctx // 2, ctx % 2, fsdp // 2, fsdp % 2
    rows, features = tokens_ref.shape
    kinds, depth, share = weight_ref.shape
    own = share // line
    flen = filter_ref.shape[1]
    begin = pl.multiple_of(z * own, own)
    groups = own // group_width
    fold = LANE // group_width
    half, quarter = rows // 2, rows // 4
    last = line - 1

    here = (ctx, fsdp)
    beside_y = (z * 2 + 1 - y, fsdp)
    beside_x = (ctx, (1 - x) * 2 + core)
    beside_core = (ctx, x * 2 + 1 - core)

    def level(at):
        return (at * 2 + y, fsdp)

    def remote(source, target, sent, received, device):
        return pltpu.make_async_remote_copy(
            src_ref=source, dst_ref=target, send_sem=sent, recv_sem=received,
            device_id=device, device_id_type=MESH,
        )

    peers = [
        ((z + dz) % line * 2 + y, (fsdp + df) % parts)
        for dz in range(line) for df in range(parts) if dz or df
    ]
    loads = [
        pltpu.make_async_copy(source, target, inputs.at[index])
        for index, (source, target) in enumerate((
            (tokens_hbm, tokens_ref),
            (gain_hbm.at[:, pl.ds(pl.multiple_of(fsdp * features, features), features)], gain_ref),
            (taps_hbm.at[:, :, pl.ds(begin, own)], taps_ref),
            (filter_hbm.at[pl.ds(pl.multiple_of(z * groups, groups), groups), :], filter_ref),
            (skip_hbm.at[:, pl.ds(begin, own)], skip_ref),
        ))
    ]
    for load in loads:
        load.start()
    barrier = pltpu.get_barrier_semaphore()
    for peer in peers + [beside_y]:
        pl.semaphore_signal(barrier, inc=1, device_id=peer, device_id_type=MESH)

    def x_place(part, at):
        return x_all.at[pl.ds(2 * part, 2), pl.ds(pl.multiple_of(at * rows, rows), rows), :]

    x_targets = [((z + 1) * 2 + y, fsdp), ((z - 1) * 2 + y, fsdp), beside_x, beside_core]
    part_x = (1 - x) * 2 + core

    def x_copy(kind, part, at):
        block = part * line + at
        place = x_place(part, at)
        return remote(place, place, x_send.at[kind, block], x_recv.at[block], x_targets[kind])

    def x_arrive(part, at):
        place = x_place(part, at)
        block = part * line + at
        remote(place, place, x_send.at[0, block], x_recv.at[block], here).wait_recv()

    def x_pass(at, up, down):
        if up:
            visit_when(z < last, lambda: x_copy(0, fsdp, at).start())
        if down:
            visit_when(z > 0, lambda: x_copy(1, fsdp, at).start())
        x_copy(2, fsdp, at).start()
        x_copy(3, fsdp, at).start()

    def x_step(away):
        @pl.when(z >= away)
        def _():
            x_arrive(fsdp, z - away)
            x_pass(z - away, True, False)

        @pl.when(z + away <= last)
        def _():
            x_arrive(fsdp, z + away)
            x_pass(z + away, False, True)

    def x_over(away):
        def take(at):
            x_arrive(part_x, at)
            x_copy(3, part_x, at).start()

        if away == 0:
            take(z)
        else:
            visit_when(z >= away, lambda: take(z - away))
            visit_when(z + away <= last, lambda: take(z + away))

    def piece(kind, at):
        return weight_ref.at[kind, :, pl.ds(pl.multiple_of(at * own, own), own)]

    def landing(kind, at, side):
        return w_all.at[2 * at + side, kind]

    def w_copy(kind, to):
        return remote(
            piece(kind, to), landing(kind, z, y),
            w_send.at[to, kind], w_recv.at[2 * z + y, kind], level(to),
        )

    def w_over(kind, at, mine):
        source = piece(kind, z) if mine else landing(kind, at, y)
        return remote(
            source, landing(kind, at, y),
            y_send.at[at, kind], w_recv.at[2 * at + y, kind], beside_y,
        )

    def w_arrive(kind, at, side):
        place = landing(kind, at, side)
        remote(place, place, y_send.at[at, kind], w_recv.at[2 * at + side, kind], here).wait_recv()

    others = [z + 1 - 2 * (z % 2), (z + 2) % line, last - z]

    def w_near():
        visit_when(z < last, lambda: w_copy(0, z + 1).start())
        visit_when(z > 0, lambda: w_copy(0, z - 1).start())

    def w_rest(goals):
        for step, goal in enumerate(goals):
            for kind in range(1 if step == 0 else 0, kinds):
                w_copy(kind, goal).start()

    def w_spread(away):
        visit_when(z == away, lambda: w_rest(range(away + 1, line)))
        visit_when(z == last - away, lambda: w_rest(range(last - away - 1, -1, -1)))

    def w_turn(step, kind):
        w_arrive(kind, others[step], y)
        w_over(kind, others[step], False).start()

    def w_turn_near():
        for kind in range(kinds):
            w_turn(0, kind)

    def multiply(at, side, kind_list, first=False):
        index = 2 * at + side

        def body(step, carry):
            span = pl.ds(pl.multiple_of(step * TILE, TILE), TILE)
            left = x_all[index, span, :]
            for kind in kind_list:
                part = jnp.dot(left, w_all[index, kind], preferred_element_type=jnp.float32)
                if first:
                    acc[kind, span, :] = part
                else:
                    acc[kind, span, :] += part
            return carry

        lax.fori_loop(0, rows * line // TILE, body, 0)

    s_targets = [beside_x, beside_core, (ctx, (1 - x) * 2 + 1 - core)]

    def s_copy(index):
        place = sums.at[fsdp]
        return remote(place, place, s_send.at[index], s_recv.at[fsdp], s_targets[index])

    def s_arrive(index):
        part = s_targets[index][1]
        place = sums.at[part]
        remote(place, place, s_send.at[index], s_recv.at[part], here).wait_recv()

    def o_copy(index):
        place = o_all.at[core, 1 - y] if index == 2 else o_all.at[core, y]
        source = o_all.at[core, 1 - y] if index == 2 else out_weight_ref
        device = beside_y if index == 0 else beside_core
        return remote(source, place, o_send.at[index], o_recv.at[index], device)

    def o_arrive(index):
        place = (o_all.at[core, 1 - y], o_all.at[1 - core, y], o_all.at[1 - core, 1 - y])[index]
        remote(place, place, o_send.at[index], o_recv.at[index], here).wait_recv()

    w_own = [
        pltpu.make_async_copy(piece(kind, z), landing(kind, z, y), w_local.at[kind])
        for kind in range(kinds)
    ]
    o_own = pltpu.make_async_copy(out_weight_ref, o_all.at[core, y], o_local.at[0])

    loads[0].wait()
    values = tokens_ref[...].astype(jnp.float32)
    squares = values * values
    coarse = squares.astype(jnp.bfloat16)
    fine = (squares - coarse.astype(jnp.float32)).astype(jnp.bfloat16)
    ones = jnp.ones((8, features), jnp.bfloat16)
    contract = (((1,), (1,)), ((), ()))
    total = lax.dot_general(ones, coarse, contract, preferred_element_type=jnp.float32)
    total += lax.dot_general(ones, fine, contract, preferred_element_type=jnp.float32)
    sums[fsdp] = total
    pl.semaphore_wait(barrier, len(peers) + 1)
    for index in range(3):
        s_copy(index).start()
    for kind in range(kinds):
        w_over(kind, z, True).start()
    w_near()
    for copy in w_own:
        copy.start()
    o_own.start()
    o_copy(1).start()
    for load in loads[1:]:
        load.wait()
    for index in range(3):
        s_arrive(index)
    square = sums[0]
    for part in range(1, parts):
        square = square + sums[part]
    mean = square[:1] / (features * parts)
    scale = jnp.broadcast_to(lax.rsqrt(mean + 1e-06), (LANE, rows)).T
    scale = jnp.concatenate([scale] * (features // LANE), axis=1)
    normed = (values * scale * gain_ref[...]).astype(jnp.bfloat16)
    for side in range(2):
        x_all[2 * fsdp + side, pl.ds(pl.multiple_of(z * rows, rows), rows), :] = (
            normed[:, side * depth : (side + 1) * depth]
        )
    x_pass(z, True, True)
    w_spread(0)

    flip = (
        lax.broadcasted_iota(jnp.int32, (flen, flen), 0)
        + lax.broadcasted_iota(jnp.int32, (flen, flen), 1)
    ) == flen - 1
    turned = jnp.dot(filter_ref[...], flip.astype(jnp.bfloat16), preferred_element_type=jnp.float32)
    base = jnp.concatenate([turned, jnp.zeros_like(turned)], axis=1)
    base = pltpu.roll(base, 1, 1)
    for group in range(groups):
        row = jnp.broadcast_to(base[group : group + 1, :], (flen, 2 * flen))
        band = pltpu.roll(row, 0, 1, stride=1, stride_axis=0)
        bands[pl.ds(group * flen, flen), :] = band.astype(jnp.bfloat16)
    halo_in[0] = jnp.zeros(halo_in.shape[1:], halo_in.dtype)

    edge = (z == 0) | (z == last)
    every = range(kinds)
    x_step(1)
    w_spread(1)
    x_over(0)
    x_step(2)
    w_spread(2)
    visit_when(jnp.logical_not(edge), w_turn_near)
    x_step(3)
    visit_when(edge, w_turn_near)
    for away in (1, 2, 3):
        x_over(away)
    w_turn(1, 0)
    w_turn(2, 0)
    for part in (x * 2 + 1 - core, (1 - x) * 2 + 1 - core):
        for at in range(line):
            x_arrive(part, at)
    for copy in w_own:
        copy.wait()
    multiply(z, y, every, True)
    for kind in every:
        w_arrive(kind, z, 1 - y)
    multiply(z, 1 - y, every)
    w_turn(1, 1)
    w_turn(2, 1)
    multiply(others[0], y, every)
    for kind in every:
        w_arrive(kind, others[0], 1 - y)
    multiply(others[0], 1 - y, every)
    w_turn(1, 2)
    w_turn(2, 2)
    multiply(others[1], y, every)
    multiply(others[2], y, every)
    for kind in every:
        for step in (1, 2):
            w_arrive(kind, others[step], 1 - y)
            multiply(others[step], 1 - y, (kind,))

    taps = taps_ref[...]
    skip = skip_ref[...]

    def h_copy(slab):
        return remote(
            halo_out.at[slab], halo_in.at[slab + 1],
            h_send.at[slab], h_recv.at[slab + 1], beside_y,
        )

    def h_arrive(slot):
        place = halo_in.at[slot]
        remote(place, place, h_send.at[0], h_recv.at[slot], here).wait_recv()

    def tap(index, kind):
        return taps[index, kind : kind + 1, :]

    for slab in range(line):
        start = slab * rows
        for kind in every:
            exact = acc[kind, start : start + rows, :].astype(jnp.bfloat16)
            acc[kind, start : start + rows, :] = exact.astype(jnp.float32)
            halo_out[slab, kind * 16 : (kind + 1) * 16, :] = exact[rows - 16 :]
        tails = []
        for kind in (1, 2):
            end = start + rows
            tails.append(
                tap(0, kind) * acc[kind, end - flen : end, :]
                + tap(1, kind) * acc[kind, end - flen - 1 : end - 1, :]
                + tap(2, kind) * acc[kind, end - flen - 2 : end - 2, :]
            )
        halo_out[slab, kinds * 16 :, :] = (tails[0] * tails[1]).astype(jnp.bfloat16)
        h_copy(slab).start()
    o_copy(0).start()

    lane_group = lax.broadcasted_iota(jnp.int32, (flen, LANE), 1) // group_width

    def mix(slab):
        if slab > 0:
            visit_when(y == 0, lambda: h_arrive(slab))
        visit_when(y == 1, lambda: h_arrive(slab + 1))
        start = slab * rows
        filtered = []
        for kind in every:
            ahead = halo_in[slab + y, kind * 16 : (kind + 1) * 16, :].astype(jnp.float32)
            extended = jnp.concatenate([ahead[8:], acc[kind, start : start + rows, :]], axis=0)
            filtered.append(short_conv([tap(index, kind) for index in range(3)], extended[6:]))
        gate, key_part, value_part = filtered
        product = (key_part * value_part).astype(jnp.bfloat16)
        reach = jnp.concatenate([halo_in[slab + y, kinds * 16 :, :], product], axis=0)
        for strip in range(own // LANE):
            lanes = slice(strip * LANE, (strip + 1) * LANE)
            matrix = bands[strip * fold * flen : (strip + 1) * fold * flen, :]
            for at in range(0, rows, flen):
                spread = jnp.dot(
                    matrix, reach[at : at + 2 * flen, lanes], preferred_element_type=jnp.float32
                )
                conv = spread[:flen]
                for group in range(1, fold):
                    conv = jnp.where(
                        lane_group == group, spread[group * flen : (group + 1) * flen], conv
                    )
                result = gate[at : at + flen, lanes] * (
                    conv + skip[:, lanes] * product[at : at + flen, lanes].astype(jnp.float32)
                )
                gated[
                    start + at : start + at + flen,
                    pl.ds(pl.multiple_of(z * own + strip * LANE, LANE), LANE),
                ] = result.astype(jnp.bfloat16)

    def g_place(slab, at):
        return gated.at[pl.ds(slab * rows, rows), pl.ds(pl.multiple_of(at * own, own), own)]

    def g_copy(kind, slab, at):
        place = g_place(slab, at)
        return remote(
            place, place, g_send.at[kind, slab, at], g_recv.at[slab, at], x_targets[kind]
        )

    def g_arrive(slab, at):
        place = g_place(slab, at)
        remote(place, place, g_send.at[0, slab, at], g_recv.at[slab, at], here).wait_recv()

    def g_step(slab, away):
        if away == 0:
            visit_when(z < last, lambda: g_copy(0, slab, z).start())
            visit_when(z > 0, lambda: g_copy(1, slab, z).start())
            return

        @pl.when(z >= away)
        def _():
            g_arrive(slab, z - away)
            visit_when(z < last, lambda: g_copy(0, slab, z - away).start())

        @pl.when(z + away <= last)
        def _():
            g_arrive(slab, z + away)
            visit_when(z > 0, lambda: g_copy(1, slab, z + away).start())

    def c_copy(slab):
        return remote(
            gated.at[pl.ds(pl.multiple_of(slab * rows + (1 - core) * half, half), half), :],
            gated_other.at[pl.ds(slab * half, half), :],
            c_send.at[slab], c_recv.at[slab], beside_core,
        )

    def t_copy(slab):
        return remote(
            cross_out.at[slab], cross_in.at[slab], t_send.at[slab], t_recv.at[slab], beside_x
        )

    def project(slab):
        c_copy(slab).wait_recv()
        mine = gated[pl.ds(pl.multiple_of(slab * rows + core * half, half), half), :]
        other = gated_other[pl.ds(slab * half, half), :]
        for side in range(2):
            part = jnp.dot(mine, o_all[core, side], preferred_element_type=jnp.float32)
            part += jnp.dot(other, o_all[1 - core, side], preferred_element_type=jnp.float32)
            width = part.shape[1]
            terms[:, side * width : (side + 1) * width] = part
        kept[slab] = terms[pl.ds(pl.multiple_of(x * quarter, quarter), quarter), :]
        cross_out[slab] = terms[
            pl.ds(pl.multiple_of((1 - x) * quarter, quarter), quarter), :
        ].astype(jnp.bfloat16)
        t_copy(slab).start()

    def out_place(x_from, core_from):
        start = pl.multiple_of(core_from * half + x_from * quarter, quarter)
        return out_ref.at[pl.ds(start, quarter), :]

    lands = fsdp == z

    def f_copy(slab):
        return remote(
            ready.at[slab], out_place(x, core), f_send.at[slab], f_recv.at[fsdp],
            (slab * 2 + y, z),
        )

    def f_stay(slab):
        return pltpu.make_async_copy(ready.at[slab], out_place(x, core), f_local.at[0])

    def hand_over(slab):
        t_copy(slab).wait_recv()
        ready[slab] = (kept[slab] + cross_in[slab].astype(jnp.float32)).astype(jnp.bfloat16)
        stays = lands & (z == slab)
        visit_when(stays, lambda: f_stay(slab).start())
        visit_when(jnp.logical_not(stays), lambda: f_copy(slab).start())

    for turn in range(line + 5):
        if turn < line:
            mix(turn)
            g_step(turn, 0)
        for away in range(1, line):
            if 0 <= turn - away < line:
                g_step(turn - away, away)
        if 0 <= turn - last < line:
            c_copy(turn - last).start()
        if turn == line - 1:
            o_arrive(0)
            o_copy(2).start()
            o_own.wait()
            o_arrive(1)
            o_arrive(2)
        if 0 <= turn - last - 1 < line:
            project(turn - last - 1)
        if 0 <= turn - last - 2 < line:
            hand_over(turn - last - 2)

    for source in range(parts):
        place = out_place(source // 2, source % 2)

        @pl.when(jnp.logical_not(lands & (fsdp == source)))
        def _():
            remote(ready.at[0], place, f_send.at[0], f_recv.at[source], here).wait_recv()

    for at in range(line):
        visit_when((z >= at) & (z < last), lambda: x_copy(0, fsdp, at).wait_send())
        visit_when((z <= at) & (z > 0), lambda: x_copy(1, fsdp, at).wait_send())
        x_copy(2, fsdp, at).wait_send()
        x_copy(3, fsdp, at).wait_send()
        x_copy(3, part_x, at).wait_send()
        for kind in every:
            w_over(kind, at, False).wait_send()
    for index in range(3):
        s_copy(index).wait_send()
    for kind in every:
        for step in range(3):
            w_copy(kind, others[step]).wait_send()
    visit_when(y == 0, lambda: h_arrive(line))
    for index in range(3):
        o_copy(index).wait_send()
    for slab in range(line):
        h_copy(slab).wait_send()
        c_copy(slab).wait_send()
        t_copy(slab).wait_send()
        for at in range(line):
            visit_when((z >= at) & (z < last), lambda: g_copy(0, slab, at).wait_send())
            visit_when((z <= at) & (z > 0), lambda: g_copy(1, slab, at).wait_send())
        stays = lands & (z == slab)
        visit_when(stays, lambda: f_stay(slab).wait())
        visit_when(jnp.logical_not(stays), lambda: f_copy(slab).wait_send())


ANY_SPEC = pl.BlockSpec(memory_space=pl.ANY)
DMA = pltpu.SemaphoreType.DMA


def level_plan(tokens, norm_gain, in_weight, short_filter, long_filter, skip_gain, out_weight):
    slabs, parts = lax.axis_size("ctx"), lax.axis_size("fsdp")
    line = slabs // 2
    rows, features = tokens.shape
    depth, kinds, share = in_weight.shape
    own = share // line
    flen = long_filter.shape[1]
    group_width = share // long_filter.shape[0]
    groups = own // group_width
    positions = rows * line
    columns = out_weight.shape[1]
    low, full = jnp.bfloat16, jnp.float32
    half, quarter = rows // 2, rows // 4
    return pl.pallas_call(
        functools.partial(block_kernel, group_width),
        out_shape=jax.ShapeDtypeStruct(tokens.shape, low),
        in_specs=[ANY_SPEC] * 7,
        out_specs=ANY_SPEC,
        scratch_shapes=[
            pltpu.VMEM(tokens.shape, low),
            pltpu.VMEM((1, features), full),
            pltpu.VMEM((3, kinds, own), full),
            pltpu.VMEM((groups, flen), low),
            pltpu.VMEM((1, own), full),
            pltpu.VMEM((2 * parts, positions, depth), low),
            pltpu.VMEM((slabs, kinds, depth, own), low),
            pltpu.VMEM((kinds, positions, own), full),
            pltpu.VMEM((parts, 8, rows), full),
            pltpu.VMEM((groups * flen, 2 * flen), low),
            pltpu.VMEM((line, kinds * 16 + flen, own), low),
            pltpu.VMEM((line + 1, kinds * 16 + flen, own), low),
            pltpu.VMEM((positions, share), low),
            pltpu.VMEM((positions // 2, share), low),
            pltpu.VMEM((2, 2, share, columns), low),
            pltpu.VMEM((half, 2 * columns), full),
            pltpu.VMEM((line, quarter, 2 * columns), full),
            pltpu.VMEM((line, quarter, 2 * columns), low),
            pltpu.VMEM((line, quarter, 2 * columns), low),
            pltpu.VMEM((line, quarter, 2 * columns), low),
            DMA((5,)), DMA((4, parts * line)), DMA((parts * line,)),
            DMA((3,)), DMA((parts,)),
            DMA((kinds,)), DMA((line, kinds)), DMA((line, kinds)), DMA((slabs, kinds)),
            DMA((line,)), DMA((line + 1,)),
            DMA((2, line, line)), DMA((line, line)),
            DMA((line,)), DMA((line,)),
            DMA((1,)), DMA((3,)), DMA((3,)),
            DMA((line,)), DMA((line,)),
            DMA((1,)), DMA((line,)), DMA((parts,)),
        ],
        compiler_params=pltpu.CompilerParams(
            collective_id=0, has_side_effects=True, vmem_limit_bytes=63 * 2**20
        ),
    )(
        tokens, norm_gain[None], in_weight.transpose(1, 0, 2), short_filter,
        long_filter, skip_gain[None], out_weight,
    )


def on_device(tokens, *rest):
    slabs, parts = lax.axis_size("ctx"), lax.axis_size("fsdp")
    depth, _, share = rest[1].shape
    groups, flen = rest[3].shape
    own = share // (slabs // 2)
    fits = (
        parts == 4 and slabs == 8 and tokens.shape[0] == 2 * flen and flen == LANE
        and tokens.shape[1] == 2 * depth and own % LANE == 0 and share == tokens.shape[1]
        and LANE % (share // groups) == 0 and depth * share <= 2**19
    )
    return (level_plan if fits else slab_plan)(tokens, *rest)


def solution(mesh):
    in_specs = (
        P("ctx", "fsdp"),
        P(),
        P("ctx", None, "fsdp"),
        P(None, None, "fsdp"),
        P("fsdp", None),
        P("fsdp"),
        P("fsdp", "ctx"),
    )
    out_specs = P("ctx", "fsdp")
    return jax.shard_map(
        on_device, mesh=mesh, in_specs=in_specs, out_specs=out_specs, check_vma=False
    )
```

```python
import functools

import jax
import jax.numpy as jnp
from jax import lax
from jax.experimental import pallas as pl
from jax.experimental.pallas import tpu as pltpu
from jax.sharding import PartitionSpec as P


def passed_along(block, axis, distance):
    devices = range(lax.axis_size(axis))
    route = [(i - distance, i) for i in devices if i - distance in devices]
    return lax.ppermute(block, axis, route)


def toeplitz_blocks(long_filter, row_count):
    groups = long_filter.shape[0]
    flen = long_filter.shape[1]
    window = flen + row_count - 1
    reversed_taps = long_filter[:, ::-1]
    padded = jnp.concatenate(
        [reversed_taps, jnp.zeros((groups, row_count), long_filter.dtype)], axis=1
    )
    tiled = jnp.tile(padded, (1, row_count))
    return tiled[:, : row_count * window].reshape(groups, row_count, window)


def short_conv(taps, extended):
    return taps[0] * extended[2:] + taps[1] * extended[1:-1] + taps[2] * extended[:-2]


def slab_plan(tokens, norm_gain, in_weight, short_filter, long_filter, skip_gain, out_weight):
    whole = lax.all_gather(tokens, "fsdp", axis=1, tiled=True)
    row_count = whole.shape[0]
    values = whole.astype(jnp.float32)
    mean_square = jnp.mean(values * values, axis=-1, keepdims=True)
    normed = (values * lax.rsqrt(mean_square + 1e-06) * norm_gain).astype(jnp.bfloat16)
    share = in_weight.shape[2]
    width_all = 3 * share
    weight_rows = lax.all_gather(in_weight, "ctx", axis=0, tiled=True)
    flat_rows = weight_rows.reshape(weight_rows.shape[0], width_all)
    proj = jnp.dot(normed, flat_rows, preferred_element_type=jnp.float32).astype(jnp.bfloat16)
    taps = short_filter.reshape(3, width_all)
    flen = long_filter.shape[1]
    earlier = passed_along(proj[row_count - 2 :], "ctx", 1)
    extended = jnp.concatenate([earlier, proj], axis=0).astype(jnp.float32)
    filtered = short_conv(taps, extended)
    out_gate = filtered[:, :share]
    product = (filtered[:, share : 2 * share] * filtered[:, 2 * share :]).astype(jnp.bfloat16)
    previous = passed_along(product[row_count - (flen - 1) :], "ctx", 1)
    product_ext = jnp.concatenate([previous, product], axis=0)
    groups = long_filter.shape[0]
    group_width = share // groups
    window = row_count + flen - 1
    blocks = toeplitz_blocks(long_filter, row_count)
    conv = jnp.einsum(
        "gts,sgc->tgc",
        blocks,
        product_ext.reshape(window, groups, group_width),
        preferred_element_type=jnp.float32,
    ).reshape(row_count, share)
    gated = (out_gate * (conv + skip_gain * product.astype(jnp.float32))).astype(jnp.bfloat16)
    terms = jnp.dot(
        gated,
        lax.all_gather(out_weight, "ctx", axis=1, tiled=True),
        preferred_element_type=jnp.float32,
    )
    mixed = lax.psum_scatter(terms, "fsdp", scatter_dimension=1, tiled=True).astype(jnp.bfloat16)
    return mixed


MESH = pl.DeviceIdType.MESH
LANE = 128
TILE = 256


def visit_when(condition, action):
    @pl.when(condition)
    def _():
        action()


def block_kernel(
    group_width, tokens_hbm, gain_hbm, weight_ref, taps_hbm, filter_hbm, skip_hbm, out_weight_ref,
    out_ref,
    tokens_ref, gain_ref, taps_ref, filter_ref, skip_ref, x_all, w_all, acc, sums, bands, halo_out, halo_in, gated, gated_other, o_all,
    terms, kept, cross_out, cross_in, ready,
    inputs, x_send, x_recv, s_send, s_recv, w_local, w_send, y_send, w_recv, h_send, h_recv,
    g_send, g_recv, c_send, c_recv, o_local, o_send, o_recv, t_send, t_recv,
    f_local, f_send, f_recv,
):
    ctx, fsdp = lax.axis_index("ctx"), lax.axis_index("fsdp")
    line, parts = lax.axis_size("ctx") // 2, lax.axis_size("fsdp")
    z, y, x, core = ctx // 2, ctx % 2, fsdp // 2, fsdp % 2
    rows, features = tokens_ref.shape
    kinds, depth, share = weight_ref.shape
    own = share // line
    flen = filter_ref.shape[1]
    begin = pl.multiple_of(z * own, own)
    groups = own // group_width
    fold = LANE // group_width
    half, quarter = rows // 2, rows // 4
    last = line - 1

    here = (ctx, fsdp)
    beside_y = (z * 2 + 1 - y, fsdp)
    beside_x = (ctx, (1 - x) * 2 + core)
    beside_core = (ctx, x * 2 + 1 - core)

    def level(at):
        return (at * 2 + y, fsdp)

    def remote(source, target, sent, received, device):
        return pltpu.make_async_remote_copy(
            src_ref=source, dst_ref=target, send_sem=sent, recv_sem=received,
            device_id=device, device_id_type=MESH,
        )

    peers = [
        ((z + dz) % line * 2 + y, (fsdp + df) % parts)
        for dz in range(line) for df in range(parts) if dz or df
    ]
    loads = [
        pltpu.make_async_copy(source, target, inputs.at[index])
        for index, (source, target) in enumerate((
            (tokens_hbm, tokens_ref),
            (gain_hbm.at[:, pl.ds(pl.multiple_of(fsdp * features, features), features)], gain_ref),
            (taps_hbm.at[:, :, pl.ds(begin, own)], taps_ref),
            (filter_hbm.at[pl.ds(pl.multiple_of(z * groups, groups), groups), :], filter_ref),
            (skip_hbm.at[:, pl.ds(begin, own)], skip_ref),
        ))
    ]
    for load in loads:
        load.start()
    barrier = pltpu.get_barrier_semaphore()
    for peer in peers + [beside_y]:
        pl.semaphore_signal(barrier, inc=1, device_id=peer, device_id_type=MESH)

    def x_place(part, at):
        return x_all.at[pl.ds(2 * part, 2), pl.ds(pl.multiple_of(at * rows, rows), rows), :]

    x_targets = [((z + 1) * 2 + y, fsdp), ((z - 1) * 2 + y, fsdp), beside_x, beside_core]
    part_x = (1 - x) * 2 + core

    def x_copy(kind, part, at):
        block = part * line + at
        place = x_place(part, at)
        return remote(place, place, x_send.at[kind, block], x_recv.at[block], x_targets[kind])

    def x_arrive(part, at):
        place = x_place(part, at)
        block = part * line + at
        remote(place, place, x_send.at[0, block], x_recv.at[block], here).wait_recv()

    def x_pass(at, up, down):
        if up:
            visit_when(z < last, lambda: x_copy(0, fsdp, at).start())
        if down:
            visit_when(z > 0, lambda: x_copy(1, fsdp, at).start())
        x_copy(2, fsdp, at).start()
        x_copy(3, fsdp, at).start()

    def x_step(away):
        @pl.when(z >= away)
        def _():
            x_arrive(fsdp, z - away)
            x_pass(z - away, True, False)

        @pl.when(z + away <= last)
        def _():
            x_arrive(fsdp, z + away)
            x_pass(z + away, False, True)

    def x_over(away):
        def take(at):
            x_arrive(part_x, at)
            x_copy(3, part_x, at).start()

        if away == 0:
            take(z)
        else:
            visit_when(z >= away, lambda: take(z - away))
            visit_when(z + away <= last, lambda: take(z + away))

    def piece(kind, at):
        return weight_ref.at[kind, :, pl.ds(pl.multiple_of(at * own, own), own)]

    def landing(kind, at, side):
        return w_all.at[2 * at + side, kind]

    def w_copy(kind, to):
        return remote(
            piece(kind, to), landing(kind, z, y),
            w_send.at[to, kind], w_recv.at[2 * z + y, kind], level(to),
        )

    def w_over(kind, at, mine):
        source = piece(kind, z) if mine else landing(kind, at, y)
        return remote(
            source, landing(kind, at, y),
            y_send.at[at, kind], w_recv.at[2 * at + y, kind], beside_y,
        )

    def w_arrive(kind, at, side):
        place = landing(kind, at, side)
        remote(place, place, y_send.at[at, kind], w_recv.at[2 * at + side, kind], here).wait_recv()

    others = [z + 1 - 2 * (z % 2), (z + 2) % line, last - z]

    def w_rest(goals):
        for goal in goals:
            for kind in range(kinds):
                w_copy(kind, goal).start()

    def w_spread(away):
        visit_when(z == away, lambda: w_rest(range(away + 1, line)))
        visit_when(z == last - away, lambda: w_rest(range(last - away - 1, -1, -1)))

    def w_turn(step, kind):
        w_arrive(kind, others[step], y)
        w_over(kind, others[step], False).start()

    def w_turn_near():
        for kind in range(kinds):
            w_turn(0, kind)

    def multiply(at, side, kind_list, first=False):
        index = 2 * at + side

        def body(step, carry):
            span = pl.ds(pl.multiple_of(step * TILE, TILE), TILE)
            left = x_all[index, span, :]
            for kind in kind_list:
                part = jnp.dot(left, w_all[index, kind], preferred_element_type=jnp.float32)
                if first:
                    acc[kind, span, :] = part
                else:
                    acc[kind, span, :] += part
            return carry

        lax.fori_loop(0, rows * line // TILE, body, 0)

    s_targets = [beside_x, beside_core, (ctx, (1 - x) * 2 + 1 - core)]

    def s_copy(index):
        place = sums.at[fsdp]
        return remote(place, place, s_send.at[index], s_recv.at[fsdp], s_targets[index])

    def s_arrive(index):
        part = s_targets[index][1]
        place = sums.at[part]
        remote(place, place, s_send.at[index], s_recv.at[part], here).wait_recv()

    def o_copy(index):
        place = o_all.at[core, 1 - y] if index == 2 else o_all.at[core, y]
        source = o_all.at[core, 1 - y] if index == 2 else out_weight_ref
        device = beside_y if index == 0 else beside_core
        return remote(source, place, o_send.at[index], o_recv.at[index], device)

    def o_arrive(index):
        place = (o_all.at[core, 1 - y], o_all.at[1 - core, y], o_all.at[1 - core, 1 - y])[index]
        remote(place, place, o_send.at[index], o_recv.at[index], here).wait_recv()

    w_own = [
        pltpu.make_async_copy(piece(kind, z), landing(kind, z, y), w_local.at[kind])
        for kind in range(kinds)
    ]
    o_own = pltpu.make_async_copy(out_weight_ref, o_all.at[core, y], o_local.at[0])

    loads[0].wait()
    values = tokens_ref[...].astype(jnp.float32)
    squares = values * values
    coarse = squares.astype(jnp.bfloat16)
    fine = (squares - coarse.astype(jnp.float32)).astype(jnp.bfloat16)
    ones = jnp.ones((8, features), jnp.bfloat16)
    contract = (((1,), (1,)), ((), ()))
    total = lax.dot_general(ones, coarse, contract, preferred_element_type=jnp.float32)
    total += lax.dot_general(ones, fine, contract, preferred_element_type=jnp.float32)
    sums[fsdp] = total
    pl.semaphore_wait(barrier, len(peers) + 1)
    for index in range(3):
        s_copy(index).start()
    for kind in range(kinds):
        w_over(kind, z, True).start()
    for copy in w_own:
        copy.start()
    o_own.start()
    o_copy(1).start()
    for load in loads[1:]:
        load.wait()
    for index in range(3):
        s_arrive(index)
    square = sums[0]
    for part in range(1, parts):
        square = square + sums[part]
    mean = square[:1] / (features * parts)
    scale = jnp.broadcast_to(lax.rsqrt(mean + 1e-06), (LANE, rows)).T
    scale = jnp.concatenate([scale] * (features // LANE), axis=1)
    normed = (values * scale * gain_ref[...]).astype(jnp.bfloat16)
    for side in range(2):
        x_all[2 * fsdp + side, pl.ds(pl.multiple_of(z * rows, rows), rows), :] = (
            normed[:, side * depth : (side + 1) * depth]
        )
    x_pass(z, True, True)
    w_spread(0)

    flip = (
        lax.broadcasted_iota(jnp.int32, (flen, flen), 0)
        + lax.broadcasted_iota(jnp.int32, (flen, flen), 1)
    ) == flen - 1
    turned = jnp.dot(filter_ref[...], flip.astype(jnp.bfloat16), preferred_element_type=jnp.float32)
    base = jnp.concatenate([turned, jnp.zeros_like(turned)], axis=1)
    base = pltpu.roll(base, 1, 1)
    for group in range(groups):
        row = jnp.broadcast_to(base[group : group + 1, :], (flen, 2 * flen))
        band = pltpu.roll(row, 0, 1, stride=1, stride_axis=0)
        bands[pl.ds(group * flen, flen), :] = band.astype(jnp.bfloat16)
    halo_in[0] = jnp.zeros(halo_in.shape[1:], halo_in.dtype)

    edge = (z == 0) | (z == last)
    every = range(kinds)
    x_step(1)
    w_spread(1)
    x_over(0)
    x_step(2)
    w_spread(2)
    visit_when(jnp.logical_not(edge), w_turn_near)
    x_step(3)
    visit_when(edge, w_turn_near)
    for away in (1, 2, 3):
        x_over(away)
    w_turn(2, 0)
    w_turn(2, 1)
    for part in (x * 2 + 1 - core, (1 - x) * 2 + 1 - core):
        for at in range(line):
            x_arrive(part, at)
    for copy in w_own:
        copy.wait()
    multiply(z, y, every, True)
    for kind in every:
        w_arrive(kind, z, 1 - y)
    multiply(z, 1 - y, every)
    w_turn(2, 2)
    w_turn(1, 0)
    multiply(others[0], y, every)
    for kind in every:
        w_arrive(kind, others[0], 1 - y)
    multiply(others[0], 1 - y, every)
    w_turn(1, 1)
    w_turn(1, 2)
    multiply(others[1], y, every)
    multiply(others[2], y, every)
    for kind in every:
        for step in (2, 1):
            w_arrive(kind, others[step], 1 - y)
            multiply(others[step], 1 - y, (kind,))

    taps = taps_ref[...]
    skip = skip_ref[...]

    def h_copy(slab):
        return remote(
            halo_out.at[slab], halo_in.at[slab + 1],
            h_send.at[slab], h_recv.at[slab + 1], beside_y,
        )

    def h_arrive(slot):
        place = halo_in.at[slot]
        remote(place, place, h_send.at[0], h_recv.at[slot], here).wait_recv()

    def tap(index, kind):
        return taps[index, kind : kind + 1, :]

    for slab in range(line):
        start = slab * rows
        for kind in every:
            exact = acc[kind, start : start + rows, :].astype(jnp.bfloat16)
            acc[kind, start : start + rows, :] = exact.astype(jnp.float32)
            halo_out[slab, kind * 16 : (kind + 1) * 16, :] = exact[rows - 16 :]
        tails = []
        for kind in (1, 2):
            end = start + rows
            tails.append(
                tap(0, kind) * acc[kind, end - flen : end, :]
                + tap(1, kind) * acc[kind, end - flen - 1 : end - 1, :]
                + tap(2, kind) * acc[kind, end - flen - 2 : end - 2, :]
            )
        halo_out[slab, kinds * 16 :, :] = (tails[0] * tails[1]).astype(jnp.bfloat16)
        h_copy(slab).start()
    o_copy(0).start()

    lane_group = lax.broadcasted_iota(jnp.int32, (flen, LANE), 1) // group_width

    def mix(slab):
        if slab > 0:
            visit_when(y == 0, lambda: h_arrive(slab))
        visit_when(y == 1, lambda: h_arrive(slab + 1))
        start = slab * rows
        filtered = []
        for kind in every:
            ahead = halo_in[slab + y, kind * 16 : (kind + 1) * 16, :].astype(jnp.float32)
            extended = jnp.concatenate([ahead[8:], acc[kind, start : start + rows, :]], axis=0)
            filtered.append(short_conv([tap(index, kind) for index in range(3)], extended[6:]))
        gate, key_part, value_part = filtered
        product = (key_part * value_part).astype(jnp.bfloat16)
        reach = jnp.concatenate([halo_in[slab + y, kinds * 16 :, :], product], axis=0)
        for strip in range(own // LANE):
            lanes = slice(strip * LANE, (strip + 1) * LANE)
            matrix = bands[strip * fold * flen : (strip + 1) * fold * flen, :]
            for at in range(0, rows, flen):
                spread = jnp.dot(
                    matrix, reach[at : at + 2 * flen, lanes], preferred_element_type=jnp.float32
                )
                conv = spread[:flen]
                for group in range(1, fold):
                    conv = jnp.where(
                        lane_group == group, spread[group * flen : (group + 1) * flen], conv
                    )
                result = gate[at : at + flen, lanes] * (
                    conv + skip[:, lanes] * product[at : at + flen, lanes].astype(jnp.float32)
                )
                gated[
                    start + at : start + at + flen,
                    pl.ds(pl.multiple_of(z * own + strip * LANE, LANE), LANE),
                ] = result.astype(jnp.bfloat16)

    def g_place(slab, at):
        return gated.at[pl.ds(slab * rows, rows), pl.ds(pl.multiple_of(at * own, own), own)]

    def g_copy(kind, slab, at):
        place = g_place(slab, at)
        return remote(
            place, place, g_send.at[kind, slab, at], g_recv.at[slab, at], x_targets[kind]
        )

    def g_arrive(slab, at):
        place = g_place(slab, at)
        remote(place, place, g_send.at[0, slab, at], g_recv.at[slab, at], here).wait_recv()

    def g_step(slab, away):
        if away == 0:
            visit_when(z < last, lambda: g_copy(0, slab, z).start())
            visit_when(z > 0, lambda: g_copy(1, slab, z).start())
            return

        @pl.when(z >= away)
        def _():
            g_arrive(slab, z - away)
            visit_when(z < last, lambda: g_copy(0, slab, z - away).start())

        @pl.when(z + away <= last)
        def _():
            g_arrive(slab, z + away)
            visit_when(z > 0, lambda: g_copy(1, slab, z + away).start())

    def c_copy(slab):
        return remote(
            gated.at[pl.ds(pl.multiple_of(slab * rows + (1 - core) * half, half), half), :],
            gated_other.at[pl.ds(slab * half, half), :],
            c_send.at[slab], c_recv.at[slab], beside_core,
        )

    def t_copy(slab):
        return remote(
            cross_out.at[slab], cross_in.at[slab], t_send.at[slab], t_recv.at[slab], beside_x
        )

    def project(slab):
        c_copy(slab).wait_recv()
        mine = gated[pl.ds(pl.multiple_of(slab * rows + core * half, half), half), :]
        other = gated_other[pl.ds(slab * half, half), :]
        for side in range(2):
            part = jnp.dot(mine, o_all[core, side], preferred_element_type=jnp.float32)
            part += jnp.dot(other, o_all[1 - core, side], preferred_element_type=jnp.float32)
            width = part.shape[1]
            terms[:, side * width : (side + 1) * width] = part
        kept[slab] = terms[pl.ds(pl.multiple_of(x * quarter, quarter), quarter), :]
        cross_out[slab] = terms[
            pl.ds(pl.multiple_of((1 - x) * quarter, quarter), quarter), :
        ].astype(jnp.bfloat16)
        t_copy(slab).start()

    def out_place(x_from, core_from):
        start = pl.multiple_of(core_from * half + x_from * quarter, quarter)
        return out_ref.at[pl.ds(start, quarter), :]

    lands = fsdp == z

    def f_copy(slab):
        return remote(
            ready.at[slab], out_place(x, core), f_send.at[slab], f_recv.at[fsdp],
            (slab * 2 + y, z),
        )

    def f_stay(slab):
        return pltpu.make_async_copy(ready.at[slab], out_place(x, core), f_local.at[0])

    def hand_over(slab):
        t_copy(slab).wait_recv()
        ready[slab] = (kept[slab] + cross_in[slab].astype(jnp.float32)).astype(jnp.bfloat16)
        stays = lands & (z == slab)
        visit_when(stays, lambda: f_stay(slab).start())
        visit_when(jnp.logical_not(stays), lambda: f_copy(slab).start())

    for turn in range(line + 5):
        if turn < line:
            mix(turn)
            g_step(turn, 0)
        for away in range(1, line):
            if 0 <= turn - away < line:
                g_step(turn - away, away)
        if 0 <= turn - last < line:
            c_copy(turn - last).start()
        if turn == line - 1:
            o_arrive(0)
            o_copy(2).start()
            o_own.wait()
            o_arrive(1)
            o_arrive(2)
        if 0 <= turn - last - 1 < line:
            project(turn - last - 1)
        if 0 <= turn - last - 2 < line:
            hand_over(turn - last - 2)

    for source in range(parts):
        place = out_place(source // 2, source % 2)

        @pl.when(jnp.logical_not(lands & (fsdp == source)))
        def _():
            remote(ready.at[0], place, f_send.at[0], f_recv.at[source], here).wait_recv()

    for at in range(line):
        visit_when((z >= at) & (z < last), lambda: x_copy(0, fsdp, at).wait_send())
        visit_when((z <= at) & (z > 0), lambda: x_copy(1, fsdp, at).wait_send())
        x_copy(2, fsdp, at).wait_send()
        x_copy(3, fsdp, at).wait_send()
        x_copy(3, part_x, at).wait_send()
        for kind in every:
            w_over(kind, at, False).wait_send()
    for index in range(3):
        s_copy(index).wait_send()
    for kind in every:
        for step in range(3):
            w_copy(kind, others[step]).wait_send()
    visit_when(y == 0, lambda: h_arrive(line))
    for index in range(3):
        o_copy(index).wait_send()
    for slab in range(line):
        h_copy(slab).wait_send()
        c_copy(slab).wait_send()
        t_copy(slab).wait_send()
        for at in range(line):
            visit_when((z >= at) & (z < last), lambda: g_copy(0, slab, at).wait_send())
            visit_when((z <= at) & (z > 0), lambda: g_copy(1, slab, at).wait_send())
        stays = lands & (z == slab)
        visit_when(stays, lambda: f_stay(slab).wait())
        visit_when(jnp.logical_not(stays), lambda: f_copy(slab).wait_send())


ANY_SPEC = pl.BlockSpec(memory_space=pl.ANY)
DMA = pltpu.SemaphoreType.DMA


def level_plan(tokens, norm_gain, in_weight, short_filter, long_filter, skip_gain, out_weight):
    slabs, parts = lax.axis_size("ctx"), lax.axis_size("fsdp")
    line = slabs // 2
    rows, features = tokens.shape
    depth, kinds, share = in_weight.shape
    own = share // line
    flen = long_filter.shape[1]
    group_width = share // long_filter.shape[0]
    groups = own // group_width
    positions = rows * line
    columns = out_weight.shape[1]
    low, full = jnp.bfloat16, jnp.float32
    half, quarter = rows // 2, rows // 4
    return pl.pallas_call(
        functools.partial(block_kernel, group_width),
        out_shape=jax.ShapeDtypeStruct(tokens.shape, low),
        in_specs=[ANY_SPEC] * 7,
        out_specs=ANY_SPEC,
        scratch_shapes=[
            pltpu.VMEM(tokens.shape, low),
            pltpu.VMEM((1, features), full),
            pltpu.VMEM((3, kinds, own), full),
            pltpu.VMEM((groups, flen), low),
            pltpu.VMEM((1, own), full),
            pltpu.VMEM((2 * parts, positions, depth), low),
            pltpu.VMEM((slabs, kinds, depth, own), low),
            pltpu.VMEM((kinds, positions, own), full),
            pltpu.VMEM((parts, 8, rows), full),
            pltpu.VMEM((groups * flen, 2 * flen), low),
            pltpu.VMEM((line, kinds * 16 + flen, own), low),
            pltpu.VMEM((line + 1, kinds * 16 + flen, own), low),
            pltpu.VMEM((positions, share), low),
            pltpu.VMEM((positions // 2, share), low),
            pltpu.VMEM((2, 2, share, columns), low),
            pltpu.VMEM((half, 2 * columns), full),
            pltpu.VMEM((line, quarter, 2 * columns), full),
            pltpu.VMEM((line, quarter, 2 * columns), low),
            pltpu.VMEM((line, quarter, 2 * columns), low),
            pltpu.VMEM((line, quarter, 2 * columns), low),
            DMA((5,)), DMA((4, parts * line)), DMA((parts * line,)),
            DMA((3,)), DMA((parts,)),
            DMA((kinds,)), DMA((line, kinds)), DMA((line, kinds)), DMA((slabs, kinds)),
            DMA((line,)), DMA((line + 1,)),
            DMA((2, line, line)), DMA((line, line)),
            DMA((line,)), DMA((line,)),
            DMA((1,)), DMA((3,)), DMA((3,)),
            DMA((line,)), DMA((line,)),
            DMA((1,)), DMA((line,)), DMA((parts,)),
        ],
        compiler_params=pltpu.CompilerParams(
            collective_id=0, has_side_effects=True, vmem_limit_bytes=63 * 2**20
        ),
    )(
        tokens, norm_gain[None], in_weight.transpose(1, 0, 2), short_filter,
        long_filter, skip_gain[None], out_weight,
    )


def on_device(tokens, *rest):
    slabs, parts = lax.axis_size("ctx"), lax.axis_size("fsdp")
    depth, _, share = rest[1].shape
    groups, flen = rest[3].shape
    own = share // (slabs // 2)
    fits = (
        parts == 4 and slabs == 8 and tokens.shape[0] == 2 * flen and flen == LANE
        and tokens.shape[1] == 2 * depth and own % LANE == 0 and share == tokens.shape[1]
        and LANE % (share // groups) == 0 and depth * share <= 2**19
    )
    return (level_plan if fits else slab_plan)(tokens, *rest)


def solution(mesh):
    in_specs = (
        P("ctx", "fsdp"),
        P(),
        P("ctx", None, "fsdp"),
        P(None, None, "fsdp"),
        P("fsdp", None),
        P("fsdp"),
        P("fsdp", "ctx"),
    )
    out_specs = P("ctx", "fsdp")
    return jax.shard_map(
        on_device, mesh=mesh, in_specs=in_specs, out_specs=out_specs, check_vma=False
    )
```

```python
import functools

import jax
import jax.numpy as jnp
from jax import lax
from jax.experimental import pallas as pl
from jax.experimental.pallas import tpu as pltpu
from jax.sharding import PartitionSpec as P


def passed_along(block, axis, distance):
    devices = range(lax.axis_size(axis))
    route = [(i - distance, i) for i in devices if i - distance in devices]
    return lax.ppermute(block, axis, route)


def toeplitz_blocks(long_filter, row_count):
    groups = long_filter.shape[0]
    flen = long_filter.shape[1]
    window = flen + row_count - 1
    reversed_taps = long_filter[:, ::-1]
    padded = jnp.concatenate(
        [reversed_taps, jnp.zeros((groups, row_count), long_filter.dtype)], axis=1
    )
    tiled = jnp.tile(padded, (1, row_count))
    return tiled[:, : row_count * window].reshape(groups, row_count, window)


def short_conv(taps, extended):
    return taps[0] * extended[2:] + taps[1] * extended[1:-1] + taps[2] * extended[:-2]


def slab_plan(tokens, norm_gain, in_weight, short_filter, long_filter, skip_gain, out_weight):
    whole = lax.all_gather(tokens, "fsdp", axis=1, tiled=True)
    row_count = whole.shape[0]
    values = whole.astype(jnp.float32)
    mean_square = jnp.mean(values * values, axis=-1, keepdims=True)
    normed = (values * lax.rsqrt(mean_square + 1e-06) * norm_gain).astype(jnp.bfloat16)
    share = in_weight.shape[2]
    width_all = 3 * share
    weight_rows = lax.all_gather(in_weight, "ctx", axis=0, tiled=True)
    flat_rows = weight_rows.reshape(weight_rows.shape[0], width_all)
    proj = jnp.dot(normed, flat_rows, preferred_element_type=jnp.float32).astype(jnp.bfloat16)
    taps = short_filter.reshape(3, width_all)
    flen = long_filter.shape[1]
    earlier = passed_along(proj[row_count - 2 :], "ctx", 1)
    extended = jnp.concatenate([earlier, proj], axis=0).astype(jnp.float32)
    filtered = short_conv(taps, extended)
    out_gate = filtered[:, :share]
    product = (filtered[:, share : 2 * share] * filtered[:, 2 * share :]).astype(jnp.bfloat16)
    previous = passed_along(product[row_count - (flen - 1) :], "ctx", 1)
    product_ext = jnp.concatenate([previous, product], axis=0)
    groups = long_filter.shape[0]
    group_width = share // groups
    window = row_count + flen - 1
    blocks = toeplitz_blocks(long_filter, row_count)
    conv = jnp.einsum(
        "gts,sgc->tgc",
        blocks,
        product_ext.reshape(window, groups, group_width),
        preferred_element_type=jnp.float32,
    ).reshape(row_count, share)
    gated = (out_gate * (conv + skip_gain * product.astype(jnp.float32))).astype(jnp.bfloat16)
    terms = jnp.dot(
        gated,
        lax.all_gather(out_weight, "ctx", axis=1, tiled=True),
        preferred_element_type=jnp.float32,
    )
    mixed = lax.psum_scatter(terms, "fsdp", scatter_dimension=1, tiled=True).astype(jnp.bfloat16)
    return mixed


MESH = pl.DeviceIdType.MESH
LANE = 128
TILE = 1024


def visit_when(condition, action):
    @pl.when(condition)
    def _():
        action()


SEND_ORDER = {1: [(0, 0), (0, 1)], 2: [(0, 0), (1, 0), (1, 1), (0, 1)], 3: [(2, 0), (0, 1), (0, 0), (1, 1), (1, 0), (2, 1)]}
EDGE_TURNS = {0: [(2, 0)], 3: [(0, 0)], 5: [(2, 1), (1, 0)], 8: [(0, 1)], 9: [(1, 1)]}
INNER_TURNS = {1: [(0, 1)], 2: [(1, 1)], 4: [(0, 0)], 5: [(1, 0), (2, 0)], 9: [(2, 1)]}
OUT_STOPS = {0: [2, 3], 2: [0], 10: [1]}


def block_kernel(
    group_width, tokens_hbm, gain_hbm, weight_ref, taps_hbm, filter_hbm, skip_hbm, out_weight_ref,
    out_ref,
    tokens_ref, gain_ref, taps_ref, filter_ref, skip_ref, x_all, w_all, acc, sums, bands, halo_out, halo_in, gated, gated_other, o_all,
    terms, kept, cross_out, cross_in, ready,
    inputs, x_send, x_recv, s_send, s_recv, w_local, w_send, y_send, w_recv, h_send, h_recv,
    g_send, g_recv, c_send, c_recv, o_local, o_send, o_recv, t_send, t_recv,
    f_local, f_send, f_recv,
):
    ctx, fsdp = lax.axis_index("ctx"), lax.axis_index("fsdp")
    line, parts = lax.axis_size("ctx") // 2, lax.axis_size("fsdp")
    z, y, x, core = ctx // 2, ctx % 2, fsdp // 2, fsdp % 2
    rows, features = tokens_ref.shape
    kinds, depth, share = weight_ref.shape
    own = share // line
    flen = filter_ref.shape[1]
    begin = pl.multiple_of(z * own, own)
    groups = own // group_width
    fold = LANE // group_width
    strips = own // LANE
    half, quarter = rows // 2, rows // 4
    last = line - 1

    here = (ctx, fsdp)
    beside_y = (z * 2 + 1 - y, fsdp)
    beside_x = (ctx, (1 - x) * 2 + core)
    beside_core = (ctx, x * 2 + 1 - core)

    def level(at):
        return (at * 2 + y, fsdp)

    def remote(source, target, sent, received, device):
        return pltpu.make_async_remote_copy(
            src_ref=source, dst_ref=target, send_sem=sent, recv_sem=received,
            device_id=device, device_id_type=MESH,
        )

    peers = [
        ((z + dz) % line * 2 + y, (fsdp + df) % parts)
        for dz in range(line) for df in range(parts) if dz or df
    ]
    loads = [
        pltpu.make_async_copy(source, target, inputs.at[index])
        for index, (source, target) in enumerate((
            (tokens_hbm, tokens_ref),
            (gain_hbm.at[:, pl.ds(pl.multiple_of(fsdp * features, features), features)], gain_ref),
            (taps_hbm.at[:, :, pl.ds(begin, own)], taps_ref),
            (filter_hbm.at[pl.ds(pl.multiple_of(z * groups, groups), groups), :], filter_ref),
            (skip_hbm.at[:, pl.ds(begin, own)], skip_ref),
        ))
    ]
    for load in loads:
        load.start()
    barrier = pltpu.get_barrier_semaphore()
    for peer in peers + [beside_y]:
        pl.semaphore_signal(barrier, inc=1, device_id=peer, device_id_type=MESH)

    def x_place(part, at):
        return x_all.at[pl.ds(2 * part, 2), pl.ds(pl.multiple_of(at * rows, rows), rows), :]

    x_targets = [((z + 1) * 2 + y, fsdp), ((z - 1) * 2 + y, fsdp), beside_x, beside_core]
    part_x = (1 - x) * 2 + core

    def x_copy(kind, part, at):
        block = part * line + at
        place = x_place(part, at)
        return remote(place, place, x_send.at[kind, block], x_recv.at[block], x_targets[kind])

    def x_arrive(part, at):
        place = x_place(part, at)
        block = part * line + at
        remote(place, place, x_send.at[0, block], x_recv.at[block], here).wait_recv()

    def x_pass(at, up, down):
        if up:
            visit_when(z < last, lambda: x_copy(0, fsdp, at).start())
        if down:
            visit_when(z > 0, lambda: x_copy(1, fsdp, at).start())
        x_copy(2, fsdp, at).start()
        x_copy(3, fsdp, at).start()

    def x_step(away):
        @pl.when(z >= away)
        def _():
            x_arrive(fsdp, z - away)
            x_pass(z - away, True, False)

        @pl.when(z + away <= last)
        def _():
            x_arrive(fsdp, z + away)
            x_pass(z + away, False, True)

    def x_over(away):
        def take(at):
            x_arrive(part_x, at)
            x_copy(3, part_x, at).start()

        if away == 0:
            take(z)
        else:
            visit_when(z >= away, lambda: take(z - away))
            visit_when(z + away <= last, lambda: take(z + away))

    cuts = [(kind, 1) for kind in range(kinds)]

    def piece(strip, cut, at):
        lanes = pl.ds(pl.multiple_of(at * own + strip * LANE, LANE), LANE)
        return weight_ref.at[cut[0], :, lanes]

    def landing(strip, cut, at, side):
        lanes = pl.ds(cut[0] * LANE, cut[1] * LANE)
        return w_all.at[2 * at + side, strip, :, lanes]

    def w_copy(strip, cut, to):
        return remote(
            piece(strip, cut, to), landing(strip, cut, z, y),
            w_send.at[to, strip, cut[0]], w_recv.at[2 * z + y, strip, cut[0]], level(to),
        )

    def w_over(strip, cut, at, mine):
        source = piece(strip, cut, z) if mine else landing(strip, cut, at, y)
        return remote(
            source, landing(strip, cut, at, y),
            y_send.at[at, strip, cut[0]], w_recv.at[2 * at + y, strip, cut[0]], beside_y,
        )

    def w_arrive(strip, cut, at, side):
        place = landing(strip, cut, at, side)
        remote(
            place, place, y_send.at[at, strip, cut[0]], w_recv.at[2 * at + side, strip, cut[0]], here
        ).wait_recv()

    others = [z + 1 - 2 * (z % 2), (z + 2) % line, last - z]

    def w_rest(goals):
        for away, strip in SEND_ORDER[len(goals)]:
            for cut in cuts:
                w_copy(strip, cut, goals[away]).start()

    def w_spread(away):
        above = range(away + 1, line)
        below = range(last - away - 1, -1, -1)
        if above:
            visit_when(z == away, lambda: w_rest(above))
            visit_when(z == last - away, lambda: w_rest(below))

    def w_turn(step, strip):
        for cut in cuts:
            w_arrive(strip, cut, others[step], y)
            w_over(strip, cut, others[step], False).start()

    def multiply(strip, at, side, cut, first=False):
        index = 2 * at + side

        def body(step, carry):
            span = pl.ds(pl.multiple_of(step * TILE, TILE), TILE)
            left = x_all[index, span, :]
            lanes = slice(cut[0] * LANE, (cut[0] + cut[1]) * LANE)
            part = jnp.dot(left, w_all[index, strip, :, lanes], preferred_element_type=jnp.float32)
            if first:
                acc[strip, span, lanes] = part
            else:
                acc[strip, span, lanes] += part
            return carry

        lax.fori_loop(0, rows * line // TILE, body, 0)

    def take(strip, at):
        for cut in cuts:
            w_arrive(strip, cut, at, 1 - y)
        multiply(strip, at, 1 - y, whole)

    s_targets = [beside_x, beside_core, (ctx, (1 - x) * 2 + 1 - core)]

    def s_copy(index):
        place = sums.at[fsdp]
        return remote(place, place, s_send.at[index], s_recv.at[fsdp], s_targets[index])

    def s_arrive(index):
        part = s_targets[index][1]
        place = sums.at[part]
        remote(place, place, s_send.at[index], s_recv.at[part], here).wait_recv()

    span = share // 4

    def o_over(index):
        rows_of = pl.ds(index * span, span)
        return remote(
            out_weight_ref.at[rows_of, :], o_all.at[core, y, rows_of],
            o_send.at[index], o_recv.at[index], beside_y,
        )

    def o_over_arrive(index):
        place = o_all.at[core, 1 - y, pl.ds(index * span, span)]
        remote(place, place, o_send.at[index], o_recv.at[index], here).wait_recv()

    def o_copy(side, own_half):
        place = o_all.at[core, side]
        slot = 4 if own_half else 5
        return remote(
            out_weight_ref if own_half else place, place,
            o_send.at[slot], o_recv.at[slot], beside_core,
        )

    def o_arrive(side, own_half):
        place = o_all.at[1 - core, side]
        slot = 4 if own_half else 5
        remote(place, place, o_send.at[slot], o_recv.at[slot], here).wait_recv()

    whole = (0, kinds)
    w_own = [
        pltpu.make_async_copy(
            piece(strip, cut, z), landing(strip, cut, z, y), w_local.at[strip, cut[0]]
        )
        for strip in range(strips) for cut in cuts
    ]
    o_own = pltpu.make_async_copy(out_weight_ref, o_all.at[core, y], o_local.at[0])

    loads[0].wait()
    values = tokens_ref[...].astype(jnp.float32)
    squares = values * values
    coarse = squares.astype(jnp.bfloat16)
    fine = (squares - coarse.astype(jnp.float32)).astype(jnp.bfloat16)
    ones = jnp.ones((8, features), jnp.bfloat16)
    contract = (((1,), (1,)), ((), ()))
    total = lax.dot_general(ones, coarse, contract, preferred_element_type=jnp.float32)
    total += lax.dot_general(ones, fine, contract, preferred_element_type=jnp.float32)
    sums[fsdp] = total
    pl.semaphore_wait(barrier, len(peers) + 1)
    for index in range(3):
        s_copy(index).start()
    for strip in range(strips):
        for cut in cuts:
            w_over(strip, cut, z, True).start()
    for copy in w_own:
        copy.start()
    o_own.start()
    o_copy(y, True).start()
    for load in loads[1:]:
        load.wait()
    for index in range(3):
        s_arrive(index)
    square = sums[0]
    for part in range(1, parts):
        square = square + sums[part]
    mean = square[:1] / (features * parts)
    scale = jnp.broadcast_to(lax.rsqrt(mean + 1e-06), (LANE, rows)).T
    scale = jnp.concatenate([scale] * (features // LANE), axis=1)
    normed = (values * scale * gain_ref[...]).astype(jnp.bfloat16)
    for side in range(2):
        x_all[2 * fsdp + side, pl.ds(pl.multiple_of(z * rows, rows), rows), :] = (
            normed[:, side * depth : (side + 1) * depth]
        )
    x_pass(z, True, True)
    w_spread(0)

    flip = (
        lax.broadcasted_iota(jnp.int32, (flen, flen), 0)
        + lax.broadcasted_iota(jnp.int32, (flen, flen), 1)
    ) == flen - 1
    turned = jnp.dot(filter_ref[...], flip.astype(jnp.bfloat16), preferred_element_type=jnp.float32)
    base = jnp.concatenate([turned, jnp.zeros_like(turned)], axis=1)
    base = pltpu.roll(base, 1, 1)
    for group in range(groups):
        row = jnp.broadcast_to(base[group : group + 1, :], (flen, 2 * flen))
        band = pltpu.roll(row, 0, 1, stride=1, stride_axis=0)
        bands[pl.ds(group * flen, flen), :] = band.astype(jnp.bfloat16)
    for strip in range(strips):
        halo_in[strip, 0] = jnp.zeros(halo_in.shape[2:], halo_in.dtype)

    def h_copy(slab, strip):
        return remote(
            halo_out.at[strip, slab], halo_in.at[strip, slab + 1],
            h_send.at[strip, slab], h_recv.at[strip, slab + 1], beside_y,
        )

    def h_arrive(slot, strip):
        place = halo_in.at[strip, slot]
        remote(place, place, h_send.at[strip, 0], h_recv.at[strip, slot], here).wait_recv()

    def tap(index, kind, strip):
        return taps_ref[index, kind : kind + 1, strip * LANE : (strip + 1) * LANE]

    every = range(kinds)

    def part_lanes(kind):
        return slice(kind * LANE, (kind + 1) * LANE)

    def edges(strip):
        for slab in range(line):
            start, end = slab * rows, (slab + 1) * rows
            for kind in every:
                exact = acc[strip, start:end, part_lanes(kind)].astype(jnp.bfloat16)
                acc[strip, start:end, part_lanes(kind)] = exact.astype(jnp.float32)
                halo_out[strip, slab, kind * 16 : (kind + 1) * 16, :] = exact[rows - 16 :]
            tails = []
            for kind in (1, 2):
                tails.append(
                    tap(0, kind, strip) * acc[strip, end - flen : end, part_lanes(kind)]
                    + tap(1, kind, strip) * acc[strip, end - flen - 1 : end - 1, part_lanes(kind)]
                    + tap(2, kind, strip) * acc[strip, end - flen - 2 : end - 2, part_lanes(kind)]
                )
            halo_out[strip, slab, kinds * 16 :, :] = (tails[0] * tails[1]).astype(jnp.bfloat16)
            h_copy(slab, strip).start()

    lane_group = lax.broadcasted_iota(jnp.int32, (flen, LANE), 1) // group_width

    def mix(slab, strip):
        if slab > 0:
            visit_when(y == 0, lambda: h_arrive(slab, strip))
        visit_when(y == 1, lambda: h_arrive(slab + 1, strip))
        start = slab * rows
        filtered = []
        for kind in every:
            ahead = halo_in[strip, slab + y, kind * 16 : (kind + 1) * 16, :].astype(jnp.float32)
            extended = jnp.concatenate([ahead[8:], acc[strip, start : start + rows, part_lanes(kind)]], axis=0)
            filtered.append(
                short_conv([tap(index, kind, strip) for index in range(3)], extended[6:])
            )
        gate, key_part, value_part = filtered
        product = (key_part * value_part).astype(jnp.bfloat16)
        reach = jnp.concatenate([halo_in[strip, slab + y, kinds * 16 :, :], product], axis=0)
        skip = skip_ref[:, strip * LANE : (strip + 1) * LANE]
        matrix = bands[strip * fold * flen : (strip + 1) * fold * flen, :]
        for at in range(0, rows, flen):
            spread = jnp.dot(
                matrix, reach[at : at + 2 * flen], preferred_element_type=jnp.float32
            )
            conv = spread[:flen]
            for group in range(1, fold):
                conv = jnp.where(
                    lane_group == group, spread[group * flen : (group + 1) * flen], conv
                )
            result = gate[at : at + flen] * (
                conv + skip * product[at : at + flen].astype(jnp.float32)
            )
            gated[
                start + at : start + at + flen,
                pl.ds(pl.multiple_of(z * own + strip * LANE, LANE), LANE),
            ] = result.astype(jnp.bfloat16)

    g_cuts = [(0, slab, 2) for slab in range(0, line, 2)] + [(1, slab, 1) for slab in range(line)]

    def g_place(index, at):
        strip, slab, count = g_cuts[index]
        lanes = pl.ds(pl.multiple_of(at * own + strip * LANE, LANE), LANE)
        return gated.at[pl.ds(slab * rows, count * rows), lanes]

    def g_copy(kind, index, at):
        place = g_place(index, at)
        return remote(
            place, place, g_send.at[kind, index, at], g_recv.at[index, at], x_targets[kind]
        )

    def g_arrive(index, at):
        place = g_place(index, at)
        remote(place, place, g_send.at[0, index, at], g_recv.at[index, at], here).wait_recv()

    def g_step(index, away):
        if away == 0:
            visit_when(z < last, lambda: g_copy(0, index, z).start())
            visit_when(z > 0, lambda: g_copy(1, index, z).start())
            return

        @pl.when(z >= away)
        def _():
            g_arrive(index, z - away)
            visit_when(z < last, lambda: g_copy(0, index, z - away).start())

        @pl.when(z + away <= last)
        def _():
            g_arrive(index, z + away)
            visit_when(z > 0, lambda: g_copy(1, index, z + away).start())

    def c_copy(slab):
        return remote(
            gated.at[pl.ds(pl.multiple_of(slab * rows + (1 - core) * half, half), half), :],
            gated_other.at[pl.ds(slab * half, half), :],
            c_send.at[slab], c_recv.at[slab], beside_core,
        )

    def t_copy(slab):
        return remote(
            cross_out.at[slab], cross_in.at[slab], t_send.at[slab], t_recv.at[slab], beside_x
        )

    def project(slab):
        c_copy(slab).wait_recv()
        mine = gated[pl.ds(pl.multiple_of(slab * rows + core * half, half), half), :]
        other = gated_other[pl.ds(slab * half, half), :]
        for side in range(2):
            part = jnp.dot(mine, o_all[core, side], preferred_element_type=jnp.float32)
            part += jnp.dot(other, o_all[1 - core, side], preferred_element_type=jnp.float32)
            width = part.shape[1]
            terms[:, side * width : (side + 1) * width] = part
        kept[slab] = terms[pl.ds(pl.multiple_of(x * quarter, quarter), quarter), :]
        cross_out[slab] = terms[
            pl.ds(pl.multiple_of((1 - x) * quarter, quarter), quarter), :
        ].astype(jnp.bfloat16)
        t_copy(slab).start()

    def out_place(x_from, core_from):
        start = pl.multiple_of(core_from * half + x_from * quarter, quarter)
        return out_ref.at[pl.ds(start, quarter), :]

    lands = fsdp == z

    def f_copy(slab):
        return remote(
            ready.at[slab], out_place(x, core), f_send.at[slab], f_recv.at[fsdp],
            (slab * 2 + y, z),
        )

    def f_stay(slab):
        return pltpu.make_async_copy(ready.at[slab], out_place(x, core), f_local.at[0])

    def hand_over(slab):
        t_copy(slab).wait_recv()
        ready[slab] = (kept[slab] + cross_in[slab].astype(jnp.float32)).astype(jnp.bfloat16)
        stays = lands & (z == slab)
        visit_when(stays, lambda: f_stay(slab).start())
        visit_when(jnp.logical_not(stays), lambda: f_copy(slab).start())

    edge = (z == 0) | (z == last)
    first_pieces = range(line // 2)

    def stop(index):
        def turns(plan):
            for step, strip in plan.get(index, ()):
                w_turn(step, strip)

        visit_when(edge, lambda: turns(EDGE_TURNS))
        visit_when(jnp.logical_not(edge), lambda: turns(INNER_TURNS))
        for part in OUT_STOPS.get(index, ()):
            o_over(part).start()

    x_step(1)
    w_spread(1)
    stop(0)
    x_step(2)
    w_spread(2)
    x_over(0)
    stop(1)
    x_step(3)
    stop(2)
    x_over(1)
    x_over(2)
    stop(3)
    x_over(3)
    for part in (x * 2 + 1 - core, (1 - x) * 2 + 1 - core):
        for at in range(line):
            x_arrive(part, at)
    for copy in w_own:
        copy.wait()
    for strip in range(strips):
        multiply(strip, z, y, whole, True)
        take(strip, z)
    stop(4)
    multiply(0, others[0], y, whole)
    stop(5)
    multiply(0, others[2], y, whole)
    multiply(0, others[1], y, whole)
    stop(6)
    for step in (0, 2, 1):
        take(0, others[step])
    stop(7)
    edges(0)
    stop(8)
    for slab in range(line):
        mix(slab, 0)
        if slab % 2:
            g_step(slab // 2, 0)
    stop(9)
    for step in (0, 2, 1):
        multiply(1, others[step], y, whole)
    take(1, others[0])
    for index in first_pieces:
        g_step(index, 1)
    take(1, others[2])
    take(1, others[1])
    edges(1)
    stop(10)
    for index in first_pieces:
        g_step(index, 2)

    for turn in range(line + 5):
        if turn < line:
            mix(turn, 1)
            g_step(line // 2 + turn, 0)
        if turn == 1:
            for index in first_pieces:
                g_step(index, 3)
        for away in range(1, line):
            if 0 <= turn - away < line:
                g_step(line // 2 + turn - away, away)
        if 0 <= turn - last < line:
            c_copy(turn - last).start()
        if turn == line - 1:
            for part in range(4):
                o_over_arrive(part)
            o_copy(1 - y, False).start()
            o_own.wait()
            o_arrive(y, True)
            o_arrive(1 - y, False)
        if 0 <= turn - last - 1 < line:
            project(turn - last - 1)
        if 0 <= turn - last - 2 < line:
            hand_over(turn - last - 2)

    for source in range(parts):
        place = out_place(source // 2, source % 2)

        @pl.when(jnp.logical_not(lands & (fsdp == source)))
        def _():
            remote(ready.at[0], place, f_send.at[0], f_recv.at[source], here).wait_recv()

    for at in range(line):
        visit_when((z >= at) & (z < last), lambda: x_copy(0, fsdp, at).wait_send())
        visit_when((z <= at) & (z > 0), lambda: x_copy(1, fsdp, at).wait_send())
        x_copy(2, fsdp, at).wait_send()
        x_copy(3, fsdp, at).wait_send()
        x_copy(3, part_x, at).wait_send()
        for strip in range(strips):
            for cut in cuts:
                w_over(strip, cut, at, False).wait_send()
    for index in range(3):
        s_copy(index).wait_send()
    for strip in range(strips):
        for cut in cuts:
            for step in range(3):
                w_copy(strip, cut, others[step]).wait_send()
        visit_when(y == 0, lambda: h_arrive(line, strip))
        for slab in range(line):
            h_copy(slab, strip).wait_send()
    for part in range(4):
        o_over(part).wait_send()
    o_copy(y, True).wait_send()
    o_copy(1 - y, False).wait_send()
    for index in range(len(g_cuts)):
        for at in range(line):
            visit_when((z >= at) & (z < last), lambda: g_copy(0, index, at).wait_send())
            visit_when((z <= at) & (z > 0), lambda: g_copy(1, index, at).wait_send())
    for slab in range(line):
        c_copy(slab).wait_send()
        t_copy(slab).wait_send()
        stays = lands & (z == slab)
        visit_when(stays, lambda: f_stay(slab).wait())
        visit_when(jnp.logical_not(stays), lambda: f_copy(slab).wait_send())


ANY_SPEC = pl.BlockSpec(memory_space=pl.ANY)
DMA = pltpu.SemaphoreType.DMA


def level_plan(tokens, norm_gain, in_weight, short_filter, long_filter, skip_gain, out_weight):
    slabs, parts = lax.axis_size("ctx"), lax.axis_size("fsdp")
    line = slabs // 2
    rows, features = tokens.shape
    depth, kinds, share = in_weight.shape
    own = share // line
    flen = long_filter.shape[1]
    group_width = share // long_filter.shape[0]
    groups = own // group_width
    strips = own // LANE
    pieces = line // 2 + line
    positions = rows * line
    columns = out_weight.shape[1]
    low, full = jnp.bfloat16, jnp.float32
    half, quarter = rows // 2, rows // 4
    return pl.pallas_call(
        functools.partial(block_kernel, group_width),
        out_shape=jax.ShapeDtypeStruct(tokens.shape, low),
        in_specs=[ANY_SPEC] * 7,
        out_specs=ANY_SPEC,
        scratch_shapes=[
            pltpu.VMEM(tokens.shape, low),
            pltpu.VMEM((1, features), full),
            pltpu.VMEM((3, kinds, own), full),
            pltpu.VMEM((groups, flen), low),
            pltpu.VMEM((1, own), full),
            pltpu.VMEM((2 * parts, positions, depth), low),
            pltpu.VMEM((slabs, strips, depth, kinds * LANE), low),
            pltpu.VMEM((strips, positions, kinds * LANE), full),
            pltpu.VMEM((parts, 8, rows), full),
            pltpu.VMEM((groups * flen, 2 * flen), low),
            pltpu.VMEM((strips, line, kinds * 16 + flen, LANE), low),
            pltpu.VMEM((strips, line + 1, kinds * 16 + flen, LANE), low),
            pltpu.VMEM((positions, share), low),
            pltpu.VMEM((positions // 2, share), low),
            pltpu.VMEM((2, 2, share, columns), low),
            pltpu.VMEM((half, 2 * columns), full),
            pltpu.VMEM((line, quarter, 2 * columns), full),
            pltpu.VMEM((line, quarter, 2 * columns), low),
            pltpu.VMEM((line, quarter, 2 * columns), low),
            pltpu.VMEM((line, quarter, 2 * columns), low),
            DMA((5,)), DMA((4, parts * line)), DMA((parts * line,)),
            DMA((3,)), DMA((parts,)),
            DMA((strips, kinds)), DMA((line, strips, kinds)), DMA((line, strips, kinds)),
            DMA((slabs, strips, kinds)),
            DMA((strips, line)), DMA((strips, line + 1)),
            DMA((2, pieces, line)), DMA((pieces, line)),
            DMA((line,)), DMA((line,)),
            DMA((1,)), DMA((6,)), DMA((6,)),
            DMA((line,)), DMA((line,)),
            DMA((1,)), DMA((line,)), DMA((parts,)),
        ],
        compiler_params=pltpu.CompilerParams(
            collective_id=0, has_side_effects=True, vmem_limit_bytes=63 * 2**20
        ),
    )(
        tokens, norm_gain[None], in_weight.transpose(1, 0, 2), short_filter,
        long_filter, skip_gain[None], out_weight,
    )


def on_device(tokens, *rest):
    slabs, parts = lax.axis_size("ctx"), lax.axis_size("fsdp")
    depth, _, share = rest[1].shape
    groups, flen = rest[3].shape
    own = share // (slabs // 2)
    fits = (
        parts == 4 and slabs == 8 and tokens.shape[0] == 2 * flen and flen == LANE
        and tokens.shape[1] == 2 * depth and own == 2 * LANE and 2 * rest[5].shape[1] == share and share == tokens.shape[1]
        and LANE % (share // groups) == 0 and depth * share <= 2**19
    )
    return (level_plan if fits else slab_plan)(tokens, *rest)


def solution(mesh):
    in_specs = (
        P("ctx", "fsdp"),
        P(),
        P("ctx", None, "fsdp"),
        P(None, None, "fsdp"),
        P("fsdp", None),
        P("fsdp"),
        P("fsdp", "ctx"),
    )
    out_specs = P("ctx", "fsdp")
    return jax.shard_map(
        on_device, mesh=mesh, in_specs=in_specs, out_specs=out_specs, check_vma=False
    )
```

```python
import functools

import jax
import jax.numpy as jnp
from jax import lax
from jax.experimental import pallas as pl
from jax.experimental.pallas import tpu as pltpu
from jax.sharding import PartitionSpec as P


def passed_along(block, axis, distance):
    devices = range(lax.axis_size(axis))
    route = [(i - distance, i) for i in devices if i - distance in devices]
    return lax.ppermute(block, axis, route)


def toeplitz_blocks(long_filter, row_count):
    groups = long_filter.shape[0]
    flen = long_filter.shape[1]
    window = flen + row_count - 1
    reversed_taps = long_filter[:, ::-1]
    padded = jnp.concatenate(
        [reversed_taps, jnp.zeros((groups, row_count), long_filter.dtype)], axis=1
    )
    tiled = jnp.tile(padded, (1, row_count))
    return tiled[:, : row_count * window].reshape(groups, row_count, window)


def short_conv(taps, extended):
    return taps[0] * extended[2:] + taps[1] * extended[1:-1] + taps[2] * extended[:-2]


def slab_plan(tokens, norm_gain, in_weight, short_filter, long_filter, skip_gain, out_weight):
    whole = lax.all_gather(tokens, "fsdp", axis=1, tiled=True)
    row_count = whole.shape[0]
    values = whole.astype(jnp.float32)
    mean_square = jnp.mean(values * values, axis=-1, keepdims=True)
    normed = (values * lax.rsqrt(mean_square + 1e-06) * norm_gain).astype(jnp.bfloat16)
    share = in_weight.shape[2]
    width_all = 3 * share
    weight_rows = lax.all_gather(in_weight, "ctx", axis=0, tiled=True)
    flat_rows = weight_rows.reshape(weight_rows.shape[0], width_all)
    proj = jnp.dot(normed, flat_rows, preferred_element_type=jnp.float32).astype(jnp.bfloat16)
    taps = short_filter.reshape(3, width_all)
    flen = long_filter.shape[1]
    earlier = passed_along(proj[row_count - 2 :], "ctx", 1)
    extended = jnp.concatenate([earlier, proj], axis=0).astype(jnp.float32)
    filtered = short_conv(taps, extended)
    out_gate = filtered[:, :share]
    product = (filtered[:, share : 2 * share] * filtered[:, 2 * share :]).astype(jnp.bfloat16)
    previous = passed_along(product[row_count - (flen - 1) :], "ctx", 1)
    product_ext = jnp.concatenate([previous, product], axis=0)
    groups = long_filter.shape[0]
    group_width = share // groups
    window = row_count + flen - 1
    blocks = toeplitz_blocks(long_filter, row_count)
    conv = jnp.einsum(
        "gts,sgc->tgc",
        blocks,
        product_ext.reshape(window, groups, group_width),
        preferred_element_type=jnp.float32,
    ).reshape(row_count, share)
    gated = (out_gate * (conv + skip_gain * product.astype(jnp.float32))).astype(jnp.bfloat16)
    terms = jnp.dot(
        gated,
        lax.all_gather(out_weight, "ctx", axis=1, tiled=True),
        preferred_element_type=jnp.float32,
    )
    mixed = lax.psum_scatter(terms, "fsdp", scatter_dimension=1, tiled=True).astype(jnp.bfloat16)
    return mixed


MESH = pl.DeviceIdType.MESH
LANE = 128
TILE = 1024


def visit_when(condition, action):
    @pl.when(condition)
    def _():
        action()


SEND_ORDER = {1: [(0, 0), (0, 1)], 2: [(0, 0), (1, 0), (1, 1), (0, 1)], 3: [(2, 0), (0, 1), (0, 0), (1, 1), (1, 0), (2, 1)]}
EDGE_TURNS = {0: [(2, 0)], 3: [(0, 0)], 5: [(2, 1), (1, 0)], 8: [(0, 1)], 9: [(1, 1)]}
INNER_TURNS = {1: [(0, 1)], 2: [(1, 1)], 4: [(0, 0)], 5: [(1, 0), (2, 0)], 9: [(2, 1)]}
SLAB_ORDER = (0, 3, 1, 2)
OUT_STOPS = {0: [2, 3], 2: [0], 10: [1]}


def block_kernel(
    group_width, tokens_hbm, gain_hbm, weight_ref, taps_hbm, filter_hbm, skip_hbm, out_weight_ref,
    out_ref,
    tokens_ref, gain_ref, taps_ref, filter_ref, skip_ref, x_all, w_all, acc, sums, bands, halo_out, halo_in, gated, gated_other, o_all,
    terms, kept, cross_out, cross_in, ready,
    inputs, x_send, x_recv, s_send, s_recv, w_local, w_send, y_send, w_recv, h_send, h_recv,
    g_send, g_recv, c_send, c_recv, o_local, o_send, o_recv, t_send, t_recv,
    f_local, f_send, f_recv,
):
    ctx, fsdp = lax.axis_index("ctx"), lax.axis_index("fsdp")
    line, parts = lax.axis_size("ctx") // 2, lax.axis_size("fsdp")
    z, y, x, core = ctx // 2, ctx % 2, fsdp // 2, fsdp % 2
    rows, features = tokens_ref.shape
    kinds, depth, share = weight_ref.shape
    own = share // line
    flen = filter_ref.shape[1]
    begin = pl.multiple_of(z * own, own)
    groups = own // group_width
    fold = LANE // group_width
    strips = own // LANE
    half, quarter = rows // 2, rows // 4
    last = line - 1

    here = (ctx, fsdp)
    beside_y = (z * 2 + 1 - y, fsdp)
    beside_x = (ctx, (1 - x) * 2 + core)
    beside_core = (ctx, x * 2 + 1 - core)

    def level(at):
        return (at * 2 + y, fsdp)

    def remote(source, target, sent, received, device):
        return pltpu.make_async_remote_copy(
            src_ref=source, dst_ref=target, send_sem=sent, recv_sem=received,
            device_id=device, device_id_type=MESH,
        )

    peers = [
        ((z + dz) % line * 2 + y, (fsdp + df) % parts)
        for dz in range(line) for df in range(parts) if dz or df
    ]
    loads = [
        pltpu.make_async_copy(source, target, inputs.at[index])
        for index, (source, target) in enumerate((
            (tokens_hbm, tokens_ref),
            (gain_hbm.at[:, pl.ds(pl.multiple_of(fsdp * features, features), features)], gain_ref),
            (taps_hbm.at[:, :, pl.ds(begin, own)], taps_ref),
            (filter_hbm.at[pl.ds(pl.multiple_of(z * groups, groups), groups), :], filter_ref),
            (skip_hbm.at[:, pl.ds(begin, own)], skip_ref),
        ))
    ]
    for load in loads:
        load.start()
    barrier = pltpu.get_barrier_semaphore()
    for peer in peers + [beside_y]:
        pl.semaphore_signal(barrier, inc=1, device_id=peer, device_id_type=MESH)

    def x_place(part, at):
        return x_all.at[pl.ds(2 * part, 2), pl.ds(pl.multiple_of(at * rows, rows), rows), :]

    x_targets = [((z + 1) * 2 + y, fsdp), ((z - 1) * 2 + y, fsdp), beside_x, beside_core]
    part_x = (1 - x) * 2 + core

    def x_copy(kind, part, at):
        block = part * line + at
        place = x_place(part, at)
        return remote(place, place, x_send.at[kind, block], x_recv.at[block], x_targets[kind])

    def x_arrive(part, at):
        place = x_place(part, at)
        block = part * line + at
        remote(place, place, x_send.at[0, block], x_recv.at[block], here).wait_recv()

    def x_pass(at, up, down):
        if up:
            visit_when(z < last, lambda: x_copy(0, fsdp, at).start())
        if down:
            visit_when(z > 0, lambda: x_copy(1, fsdp, at).start())
        x_copy(2, fsdp, at).start()
        x_copy(3, fsdp, at).start()

    def x_step(away):
        @pl.when(z >= away)
        def _():
            x_arrive(fsdp, z - away)
            x_pass(z - away, True, False)

        @pl.when(z + away <= last)
        def _():
            x_arrive(fsdp, z + away)
            x_pass(z + away, False, True)

    def x_over(away):
        def take(at):
            x_arrive(part_x, at)
            x_copy(3, part_x, at).start()

        if away == 0:
            take(z)
        else:
            visit_when(z >= away, lambda: take(z - away))
            visit_when(z + away <= last, lambda: take(z + away))

    cuts = [(kind, 1) for kind in range(kinds)]

    def piece(strip, cut, at):
        lanes = pl.ds(pl.multiple_of(at * own + strip * LANE, LANE), LANE)
        return weight_ref.at[cut[0], :, lanes]

    def landing(strip, cut, at, side):
        lanes = pl.ds(cut[0] * LANE, cut[1] * LANE)
        return w_all.at[2 * at + side, strip, :, lanes]

    def w_copy(strip, cut, to):
        return remote(
            piece(strip, cut, to), landing(strip, cut, z, y),
            w_send.at[to, strip, cut[0]], w_recv.at[2 * z + y, strip, cut[0]], level(to),
        )

    def w_over(strip, cut, at, mine):
        source = piece(strip, cut, z) if mine else landing(strip, cut, at, y)
        return remote(
            source, landing(strip, cut, at, y),
            y_send.at[at, strip, cut[0]], w_recv.at[2 * at + y, strip, cut[0]], beside_y,
        )

    def w_arrive(strip, cut, at, side):
        place = landing(strip, cut, at, side)
        remote(
            place, place, y_send.at[at, strip, cut[0]], w_recv.at[2 * at + side, strip, cut[0]], here
        ).wait_recv()

    others = [z + 1 - 2 * (z % 2), (z + 2) % line, last - z]

    def w_rest(goals):
        for away, strip in SEND_ORDER[len(goals)]:
            for cut in cuts:
                w_copy(strip, cut, goals[away]).start()

    def w_spread(away):
        above = range(away + 1, line)
        below = range(last - away - 1, -1, -1)
        if above:
            visit_when(z == away, lambda: w_rest(above))
            visit_when(z == last - away, lambda: w_rest(below))

    def w_turn(step, strip):
        for cut in cuts:
            w_arrive(strip, cut, others[step], y)
            w_over(strip, cut, others[step], False).start()

    def multiply(strip, at, side, cut, first=False):
        index = 2 * at + side

        def body(step, carry):
            span = pl.ds(pl.multiple_of(step * TILE, TILE), TILE)
            left = x_all[index, span, :]
            lanes = slice(cut[0] * LANE, (cut[0] + cut[1]) * LANE)
            part = jnp.dot(left, w_all[index, strip, :, lanes], preferred_element_type=jnp.float32)
            if first:
                acc[strip, span, lanes] = part
            else:
                acc[strip, span, lanes] += part
            return carry

        lax.fori_loop(0, rows * line // TILE, body, 0)

    def take(strip, at):
        for cut in cuts:
            w_arrive(strip, cut, at, 1 - y)
        multiply(strip, at, 1 - y, whole)

    s_targets = [beside_x, beside_core, (ctx, (1 - x) * 2 + 1 - core)]

    def s_copy(index):
        place = sums.at[fsdp]
        return remote(place, place, s_send.at[index], s_recv.at[fsdp], s_targets[index])

    def s_arrive(index):
        part = s_targets[index][1]
        place = sums.at[part]
        remote(place, place, s_send.at[index], s_recv.at[part], here).wait_recv()

    span = share // 4

    def o_over(index):
        rows_of = pl.ds(index * span, span)
        return remote(
            out_weight_ref.at[rows_of, :], o_all.at[core, y, rows_of],
            o_send.at[index], o_recv.at[index], beside_y,
        )

    def o_over_arrive(index):
        place = o_all.at[core, 1 - y, pl.ds(index * span, span)]
        remote(place, place, o_send.at[index], o_recv.at[index], here).wait_recv()

    def o_copy(side, own_half):
        place = o_all.at[core, side]
        slot = 4 if own_half else 5
        return remote(
            out_weight_ref if own_half else place, place,
            o_send.at[slot], o_recv.at[slot], beside_core,
        )

    def o_arrive(side, own_half):
        place = o_all.at[1 - core, side]
        slot = 4 if own_half else 5
        remote(place, place, o_send.at[slot], o_recv.at[slot], here).wait_recv()

    whole = (0, kinds)
    w_own = [
        pltpu.make_async_copy(
            piece(strip, cut, z), landing(strip, cut, z, y), w_local.at[strip, cut[0]]
        )
        for strip in range(strips) for cut in cuts
    ]
    o_own = pltpu.make_async_copy(out_weight_ref, o_all.at[core, y], o_local.at[0])

    loads[0].wait()
    values = tokens_ref[...].astype(jnp.float32)
    squares = values * values
    coarse = squares.astype(jnp.bfloat16)
    fine = (squares - coarse.astype(jnp.float32)).astype(jnp.bfloat16)
    ones = jnp.ones((8, features), jnp.bfloat16)
    contract = (((1,), (1,)), ((), ()))
    total = lax.dot_general(ones, coarse, contract, preferred_element_type=jnp.float32)
    total += lax.dot_general(ones, fine, contract, preferred_element_type=jnp.float32)
    sums[fsdp] = total
    pl.semaphore_wait(barrier, len(peers) + 1)
    for index in range(3):
        s_copy(index).start()
    for strip in range(strips):
        for cut in cuts:
            w_over(strip, cut, z, True).start()
    for copy in w_own:
        copy.start()
    o_own.start()
    o_copy(y, True).start()
    for load in loads[1:]:
        load.wait()
    for index in range(3):
        s_arrive(index)
    square = sums[0]
    for part in range(1, parts):
        square = square + sums[part]
    mean = square[:1] / (features * parts)
    scale = jnp.broadcast_to(lax.rsqrt(mean + 1e-06), (LANE, rows)).T
    scale = jnp.concatenate([scale] * (features // LANE), axis=1)
    normed = (values * scale * gain_ref[...]).astype(jnp.bfloat16)
    for side in range(2):
        x_all[2 * fsdp + side, pl.ds(pl.multiple_of(z * rows, rows), rows), :] = (
            normed[:, side * depth : (side + 1) * depth]
        )
    x_pass(z, True, True)
    w_spread(0)

    flip = (
        lax.broadcasted_iota(jnp.int32, (flen, flen), 0)
        + lax.broadcasted_iota(jnp.int32, (flen, flen), 1)
    ) == flen - 1
    turned = jnp.dot(filter_ref[...], flip.astype(jnp.bfloat16), preferred_element_type=jnp.float32)
    base = jnp.concatenate([turned, jnp.zeros_like(turned)], axis=1)
    base = pltpu.roll(base, 1, 1)
    for group in range(groups):
        row = jnp.broadcast_to(base[group : group + 1, :], (flen, 2 * flen))
        band = pltpu.roll(row, 0, 1, stride=1, stride_axis=0)
        bands[pl.ds(group * flen, flen), :] = band.astype(jnp.bfloat16)
    for strip in range(strips):
        halo_in[strip, 0] = jnp.zeros(halo_in.shape[2:], halo_in.dtype)

    def h_copy(slab, strip):
        return remote(
            halo_out.at[strip, slab], halo_in.at[strip, slab + 1],
            h_send.at[strip, slab], h_recv.at[strip, slab + 1], beside_y,
        )

    def h_arrive(slot, strip):
        place = halo_in.at[strip, slot]
        remote(place, place, h_send.at[strip, 0], h_recv.at[strip, slot], here).wait_recv()

    def tap(index, kind, strip):
        return taps_ref[index, kind : kind + 1, strip * LANE : (strip + 1) * LANE]

    every = range(kinds)

    def part_lanes(kind):
        return slice(kind * LANE, (kind + 1) * LANE)

    def edges(strip):
        for slab in range(line):
            start, end = slab * rows, (slab + 1) * rows
            for kind in every:
                exact = acc[strip, start:end, part_lanes(kind)].astype(jnp.bfloat16)
                acc[strip, start:end, part_lanes(kind)] = exact.astype(jnp.float32)
                halo_out[strip, slab, kind * 16 : (kind + 1) * 16, :] = exact[rows - 16 :]
            tails = []
            for kind in (1, 2):
                tails.append(
                    tap(0, kind, strip) * acc[strip, end - flen : end, part_lanes(kind)]
                    + tap(1, kind, strip) * acc[strip, end - flen - 1 : end - 1, part_lanes(kind)]
                    + tap(2, kind, strip) * acc[strip, end - flen - 2 : end - 2, part_lanes(kind)]
                )
            halo_out[strip, slab, kinds * 16 :, :] = (tails[0] * tails[1]).astype(jnp.bfloat16)
            h_copy(slab, strip).start()

    lane_group = lax.broadcasted_iota(jnp.int32, (flen, LANE), 1) // group_width

    def mix(slab, strip):
        if slab > 0:
            visit_when(y == 0, lambda: h_arrive(slab, strip))
        visit_when(y == 1, lambda: h_arrive(slab + 1, strip))
        start = slab * rows
        filtered = []
        for kind in every:
            ahead = halo_in[strip, slab + y, kind * 16 : (kind + 1) * 16, :].astype(jnp.float32)
            extended = jnp.concatenate([ahead[8:], acc[strip, start : start + rows, part_lanes(kind)]], axis=0)
            filtered.append(
                short_conv([tap(index, kind, strip) for index in range(3)], extended[6:])
            )
        gate, key_part, value_part = filtered
        product = (key_part * value_part).astype(jnp.bfloat16)
        reach = jnp.concatenate([halo_in[strip, slab + y, kinds * 16 :, :], product], axis=0)
        skip = skip_ref[:, strip * LANE : (strip + 1) * LANE]
        matrix = bands[strip * fold * flen : (strip + 1) * fold * flen, :]
        for at in range(0, rows, flen):
            spread = jnp.dot(
                matrix, reach[at : at + 2 * flen], preferred_element_type=jnp.float32
            )
            conv = spread[:flen]
            for group in range(1, fold):
                conv = jnp.where(
                    lane_group == group, spread[group * flen : (group + 1) * flen], conv
                )
            result = gate[at : at + flen] * (
                conv + skip * product[at : at + flen].astype(jnp.float32)
            )
            gated[
                start + at : start + at + flen,
                pl.ds(pl.multiple_of(z * own + strip * LANE, LANE), LANE),
            ] = result.astype(jnp.bfloat16)

    g_cuts = [(0, slab, 2) for slab in range(0, line, 2)] + [(1, slab, 1) for slab in range(line)]

    def g_place(index, at):
        strip, slab, count = g_cuts[index]
        lanes = pl.ds(pl.multiple_of(at * own + strip * LANE, LANE), LANE)
        return gated.at[pl.ds(slab * rows, count * rows), lanes]

    def g_copy(kind, index, at):
        place = g_place(index, at)
        return remote(
            place, place, g_send.at[kind, index, at], g_recv.at[index, at], x_targets[kind]
        )

    def g_arrive(index, at):
        place = g_place(index, at)
        remote(place, place, g_send.at[0, index, at], g_recv.at[index, at], here).wait_recv()

    def g_step(index, away):
        if away == 0:
            visit_when(z < last, lambda: g_copy(0, index, z).start())
            visit_when(z > 0, lambda: g_copy(1, index, z).start())
            return

        @pl.when(z >= away)
        def _():
            g_arrive(index, z - away)
            visit_when(z < last, lambda: g_copy(0, index, z - away).start())

        @pl.when(z + away <= last)
        def _():
            g_arrive(index, z + away)
            visit_when(z > 0, lambda: g_copy(1, index, z + away).start())

    def c_copy(slab):
        return remote(
            gated.at[pl.ds(pl.multiple_of(slab * rows + (1 - core) * half, half), half), :],
            gated_other.at[pl.ds(slab * half, half), :],
            c_send.at[slab], c_recv.at[slab], beside_core,
        )

    def t_copy(slab, side):
        return remote(
            cross_out.at[slab, side], cross_in.at[slab, side],
            t_send.at[slab, side], t_recv.at[slab, side], beside_x,
        )

    def project(slab):
        c_copy(slab).wait_recv()
        mine = gated[pl.ds(pl.multiple_of(slab * rows + core * half, half), half), :]
        other = gated_other[pl.ds(slab * half, half), :]
        for side in range(2):
            part = jnp.dot(mine, o_all[core, side], preferred_element_type=jnp.float32)
            part += jnp.dot(other, o_all[1 - core, side], preferred_element_type=jnp.float32)
            terms[side] = part
            kept[slab, side] = terms[side, pl.ds(pl.multiple_of(x * quarter, quarter), quarter), :]
            cross_out[slab, side] = terms[
                side, pl.ds(pl.multiple_of((1 - x) * quarter, quarter), quarter), :
            ].astype(jnp.bfloat16)
            t_copy(slab, side).start()

    def out_place(x_from, core_from, side):
        start = pl.multiple_of(core_from * half + x_from * quarter, quarter)
        width = out_weight_ref.shape[1]
        return out_ref.at[pl.ds(start, quarter), pl.ds(side * width, width)]

    lands = fsdp == z

    def f_copy(slab, side):
        return remote(
            ready.at[slab, side], out_place(x, core, side),
            f_send.at[slab, side], f_recv.at[fsdp, side], (slab * 2 + y, z),
        )

    def f_stay(slab, side):
        return pltpu.make_async_copy(
            ready.at[slab, side], out_place(x, core, side), f_local.at[side]
        )

    def hand_over(slab):
        stays = lands & (z == slab)
        for side in range(2):
            t_copy(slab, side).wait_recv()
            ready[slab, side] = (
                kept[slab, side] + cross_in[slab, side].astype(jnp.float32)
            ).astype(jnp.bfloat16)
            visit_when(stays, lambda: f_stay(slab, side).start())
            visit_when(jnp.logical_not(stays), lambda: f_copy(slab, side).start())

    edge = (z == 0) | (z == last)
    first_pieces = range(line // 2)

    def stop(index):
        def turns(plan):
            for step, strip in plan.get(index, ()):
                w_turn(step, strip)

        visit_when(edge, lambda: turns(EDGE_TURNS))
        visit_when(jnp.logical_not(edge), lambda: turns(INNER_TURNS))
        for part in OUT_STOPS.get(index, ()):
            o_over(part).start()

    x_step(1)
    w_spread(1)
    stop(0)
    x_step(2)
    w_spread(2)
    x_over(0)
    stop(1)
    x_step(3)
    stop(2)
    x_over(1)
    x_over(2)
    stop(3)
    x_over(3)
    for part in (x * 2 + 1 - core, (1 - x) * 2 + 1 - core):
        for at in range(line):
            x_arrive(part, at)
    for copy in w_own:
        copy.wait()
    for strip in range(strips):
        multiply(strip, z, y, whole, True)
        take(strip, z)
    stop(4)
    multiply(0, others[0], y, whole)
    stop(5)
    multiply(0, others[2], y, whole)
    multiply(0, others[1], y, whole)
    stop(6)
    for step in (0, 2, 1):
        take(0, others[step])
    stop(7)
    edges(0)
    stop(8)
    for slab in range(line):
        mix(slab, 0)
        if slab % 2:
            g_step(slab // 2, 0)
    stop(9)
    for step in (0, 2, 1):
        multiply(1, others[step], y, whole)
    take(1, others[0])
    for index in first_pieces:
        g_step(index, 1)
    take(1, others[2])
    take(1, others[1])
    edges(1)
    stop(10)
    for index in first_pieces:
        g_step(index, 2)

    def slab_at(turn):
        return SLAB_ORDER[turn] if 0 <= turn < line else None

    for turn in range(line + 5):
        if turn < line:
            mix(slab_at(turn), 1)
            g_step(line // 2 + slab_at(turn), 0)
        if turn == 1:
            for index in first_pieces:
                g_step(index, 3)
        for away in range(1, line):
            slab = slab_at(turn - away)
            if slab is not None:
                g_step(line // 2 + slab, away)
        slab = slab_at(turn - last)
        if slab is not None:
            c_copy(slab).start()
        if turn == line - 1:
            for part in range(4):
                o_over_arrive(part)
            o_copy(1 - y, False).start()
            o_own.wait()
            o_arrive(y, True)
            o_arrive(1 - y, False)
        slab = slab_at(turn - last - 1)
        if slab is not None:
            project(slab)
        slab = slab_at(turn - last - 2)
        if slab is not None:
            hand_over(slab)

    for source in range(parts):
        @pl.when(jnp.logical_not(lands & (fsdp == source)))
        def _():
            for side in range(2):
                place = out_place(source // 2, source % 2, side)
                remote(
                    ready.at[0, side], place, f_send.at[0, side], f_recv.at[source, side], here
                ).wait_recv()

    for at in range(line):
        visit_when((z >= at) & (z < last), lambda: x_copy(0, fsdp, at).wait_send())
        visit_when((z <= at) & (z > 0), lambda: x_copy(1, fsdp, at).wait_send())
        x_copy(2, fsdp, at).wait_send()
        x_copy(3, fsdp, at).wait_send()
        x_copy(3, part_x, at).wait_send()
        for strip in range(strips):
            for cut in cuts:
                w_over(strip, cut, at, False).wait_send()
    for index in range(3):
        s_copy(index).wait_send()
    for strip in range(strips):
        for cut in cuts:
            for step in range(3):
                w_copy(strip, cut, others[step]).wait_send()
        visit_when(y == 0, lambda: h_arrive(line, strip))
        for slab in range(line):
            h_copy(slab, strip).wait_send()
    for part in range(4):
        o_over(part).wait_send()
    o_copy(y, True).wait_send()
    o_copy(1 - y, False).wait_send()
    for index in range(len(g_cuts)):
        for at in range(line):
            visit_when((z >= at) & (z < last), lambda: g_copy(0, index, at).wait_send())
            visit_when((z <= at) & (z > 0), lambda: g_copy(1, index, at).wait_send())
    for slab in range(line):
        c_copy(slab).wait_send()
        for side in range(2):
            t_copy(slab, side).wait_send()
        stays = lands & (z == slab)
        for side in range(2):
            visit_when(stays, lambda: f_stay(slab, side).wait())
            visit_when(jnp.logical_not(stays), lambda: f_copy(slab, side).wait_send())


ANY_SPEC = pl.BlockSpec(memory_space=pl.ANY)
DMA = pltpu.SemaphoreType.DMA


def level_plan(tokens, norm_gain, in_weight, short_filter, long_filter, skip_gain, out_weight):
    slabs, parts = lax.axis_size("ctx"), lax.axis_size("fsdp")
    line = slabs // 2
    rows, features = tokens.shape
    depth, kinds, share = in_weight.shape
    own = share // line
    flen = long_filter.shape[1]
    group_width = share // long_filter.shape[0]
    groups = own // group_width
    strips = own // LANE
    pieces = line // 2 + line
    positions = rows * line
    columns = out_weight.shape[1]
    low, full = jnp.bfloat16, jnp.float32
    half, quarter = rows // 2, rows // 4
    return pl.pallas_call(
        functools.partial(block_kernel, group_width),
        out_shape=jax.ShapeDtypeStruct(tokens.shape, low),
        in_specs=[ANY_SPEC] * 7,
        out_specs=ANY_SPEC,
        scratch_shapes=[
            pltpu.VMEM(tokens.shape, low),
            pltpu.VMEM((1, features), full),
            pltpu.VMEM((3, kinds, own), full),
            pltpu.VMEM((groups, flen), low),
            pltpu.VMEM((1, own), full),
            pltpu.VMEM((2 * parts, positions, depth), low),
            pltpu.VMEM((slabs, strips, depth, kinds * LANE), low),
            pltpu.VMEM((strips, positions, kinds * LANE), full),
            pltpu.VMEM((parts, 8, rows), full),
            pltpu.VMEM((groups * flen, 2 * flen), low),
            pltpu.VMEM((strips, line, kinds * 16 + flen, LANE), low),
            pltpu.VMEM((strips, line + 1, kinds * 16 + flen, LANE), low),
            pltpu.VMEM((positions, share), low),
            pltpu.VMEM((positions // 2, share), low),
            pltpu.VMEM((2, 2, share, columns), low),
            pltpu.VMEM((2, half, columns), full),
            pltpu.VMEM((line, 2, quarter, columns), full),
            pltpu.VMEM((line, 2, quarter, columns), low),
            pltpu.VMEM((line, 2, quarter, columns), low),
            pltpu.VMEM((line, 2, quarter, columns), low),
            DMA((5,)), DMA((4, parts * line)), DMA((parts * line,)),
            DMA((3,)), DMA((parts,)),
            DMA((strips, kinds)), DMA((line, strips, kinds)), DMA((line, strips, kinds)),
            DMA((slabs, strips, kinds)),
            DMA((strips, line)), DMA((strips, line + 1)),
            DMA((2, pieces, line)), DMA((pieces, line)),
            DMA((line,)), DMA((line,)),
            DMA((1,)), DMA((6,)), DMA((6,)),
            DMA((line, 2)), DMA((line, 2)),
            DMA((2,)), DMA((line, 2)), DMA((parts, 2)),
        ],
        compiler_params=pltpu.CompilerParams(
            collective_id=0, has_side_effects=True, vmem_limit_bytes=63 * 2**20
        ),
    )(
        tokens, norm_gain[None], in_weight.transpose(1, 0, 2), short_filter,
        long_filter, skip_gain[None], out_weight,
    )


def on_device(tokens, *rest):
    slabs, parts = lax.axis_size("ctx"), lax.axis_size("fsdp")
    depth, _, share = rest[1].shape
    groups, flen = rest[3].shape
    own = share // (slabs // 2)
    fits = (
        parts == 4 and slabs == 8 and tokens.shape[0] == 2 * flen and flen == LANE
        and tokens.shape[1] == 2 * depth and own == 2 * LANE and 2 * rest[5].shape[1] == share and share == tokens.shape[1]
        and LANE % (share // groups) == 0 and depth * share <= 2**19
    )
    return (level_plan if fits else slab_plan)(tokens, *rest)


def solution(mesh):
    in_specs = (
        P("ctx", "fsdp"),
        P(),
        P("ctx", None, "fsdp"),
        P(None, None, "fsdp"),
        P("fsdp", None),
        P("fsdp"),
        P("fsdp", "ctx"),
    )
    out_specs = P("ctx", "fsdp")
    return jax.shard_map(
        on_device, mesh=mesh, in_specs=in_specs, out_specs=out_specs, check_vma=False
    )
```

```python
import functools

import jax
import jax.numpy as jnp
from jax import lax
from jax.experimental import pallas as pl
from jax.experimental.pallas import tpu as pltpu
from jax.sharding import PartitionSpec as P


def passed_along(block, axis, distance):
    devices = range(lax.axis_size(axis))
    route = [(i - distance, i) for i in devices if i - distance in devices]
    return lax.ppermute(block, axis, route)


def toeplitz_blocks(long_filter, row_count):
    groups = long_filter.shape[0]
    flen = long_filter.shape[1]
    window = flen + row_count - 1
    reversed_taps = long_filter[:, ::-1]
    padded = jnp.concatenate(
        [reversed_taps, jnp.zeros((groups, row_count), long_filter.dtype)], axis=1
    )
    tiled = jnp.tile(padded, (1, row_count))
    return tiled[:, : row_count * window].reshape(groups, row_count, window)


def short_conv(taps, extended):
    return taps[0] * extended[2:] + taps[1] * extended[1:-1] + taps[2] * extended[:-2]


def slab_plan(tokens, norm_gain, in_weight, short_filter, long_filter, skip_gain, out_weight):
    whole = lax.all_gather(tokens, "fsdp", axis=1, tiled=True)
    row_count = whole.shape[0]
    values = whole.astype(jnp.float32)
    mean_square = jnp.mean(values * values, axis=-1, keepdims=True)
    normed = (values * lax.rsqrt(mean_square + 1e-06) * norm_gain).astype(jnp.bfloat16)
    share = in_weight.shape[2]
    width_all = 3 * share
    weight_rows = lax.all_gather(in_weight, "ctx", axis=0, tiled=True)
    flat_rows = weight_rows.reshape(weight_rows.shape[0], width_all)
    proj = jnp.dot(normed, flat_rows, preferred_element_type=jnp.float32).astype(jnp.bfloat16)
    taps = short_filter.reshape(3, width_all)
    flen = long_filter.shape[1]
    earlier = passed_along(proj[row_count - 2 :], "ctx", 1)
    extended = jnp.concatenate([earlier, proj], axis=0).astype(jnp.float32)
    filtered = short_conv(taps, extended)
    out_gate = filtered[:, :share]
    product = (filtered[:, share : 2 * share] * filtered[:, 2 * share :]).astype(jnp.bfloat16)
    previous = passed_along(product[row_count - (flen - 1) :], "ctx", 1)
    product_ext = jnp.concatenate([previous, product], axis=0)
    groups = long_filter.shape[0]
    group_width = share // groups
    window = row_count + flen - 1
    blocks = toeplitz_blocks(long_filter, row_count)
    conv = jnp.einsum(
        "gts,sgc->tgc",
        blocks,
        product_ext.reshape(window, groups, group_width),
        preferred_element_type=jnp.float32,
    ).reshape(row_count, share)
    gated = (out_gate * (conv + skip_gain * product.astype(jnp.float32))).astype(jnp.bfloat16)
    terms = jnp.dot(
        gated,
        lax.all_gather(out_weight, "ctx", axis=1, tiled=True),
        preferred_element_type=jnp.float32,
    )
    mixed = lax.psum_scatter(terms, "fsdp", scatter_dimension=1, tiled=True).astype(jnp.bfloat16)
    return mixed


MESH = pl.DeviceIdType.MESH
LANE = 128
TILE = 1024


def visit_when(condition, action):
    @pl.when(condition)
    def _():
        action()


SEND_ORDER = {1: [(0, 0), (0, 1)], 2: [(0, 0), (1, 0), (1, 1), (0, 1)], 3: [(2, 0), (0, 1), (0, 0), (1, 1), (1, 0), (2, 1)]}
SEND_EARLY = {1: 0, 2: 0, 3: 1}
EDGE_TURNS = {0: [(2, 0)], 3: [(0, 0)], 5: [(2, 1), (1, 0)], 8: [(0, 1)], 9: [(1, 1)]}
INNER_TURNS = {1: [(0, 1)], 2: [(1, 1)], 4: [(0, 0)], 5: [(1, 0), (2, 0)], 9: [(2, 1)]}
SLAB_ORDER = (0, 3, 1, 2)
OUT_STOPS = {0: [2, 3], 2: [0], 10: [1]}


def block_kernel(
    group_width, tokens_hbm, gain_hbm, weight_ref, taps_hbm, filter_hbm, skip_hbm, out_weight_ref,
    out_ref,
    tokens_ref, gain_ref, taps_ref, filter_ref, skip_ref, x_all, w_all, acc, sums, bands, halo_out, halo_in, gated, gated_other, o_all,
    terms, kept, cross_out, cross_in, ready,
    inputs, x_send, x_recv, s_send, s_recv, w_local, w_send, y_send, w_recv, h_send, h_recv,
    g_send, g_recv, c_send, c_recv, o_local, o_send, o_recv, t_send, t_recv,
    f_local, f_send, f_recv,
):
    ctx, fsdp = lax.axis_index("ctx"), lax.axis_index("fsdp")
    line, parts = lax.axis_size("ctx") // 2, lax.axis_size("fsdp")
    z, y, x, core = ctx // 2, ctx % 2, fsdp // 2, fsdp % 2
    rows, features = tokens_ref.shape
    kinds, depth, share = weight_ref.shape
    own = share // line
    flen = filter_ref.shape[1]
    begin = pl.multiple_of(z * own, own)
    groups = own // group_width
    fold = LANE // group_width
    strips = own // LANE
    half, quarter = rows // 2, rows // 4
    last = line - 1

    here = (ctx, fsdp)
    beside_y = (z * 2 + 1 - y, fsdp)
    beside_x = (ctx, (1 - x) * 2 + core)
    beside_core = (ctx, x * 2 + 1 - core)

    def level(at):
        return (at * 2 + y, fsdp)

    def remote(source, target, sent, received, device):
        return pltpu.make_async_remote_copy(
            src_ref=source, dst_ref=target, send_sem=sent, recv_sem=received,
            device_id=device, device_id_type=MESH,
        )

    peers = [
        ((z + dz) % line * 2 + y, (fsdp + df) % parts)
        for dz in range(line) for df in range(parts) if dz or df
    ]
    loads = [
        pltpu.make_async_copy(source, target, inputs.at[index])
        for index, (source, target) in enumerate((
            (tokens_hbm, tokens_ref),
            (gain_hbm.at[:, pl.ds(pl.multiple_of(fsdp * features, features), features)], gain_ref),
            (taps_hbm.at[:, :, pl.ds(begin, own)], taps_ref),
            (filter_hbm.at[pl.ds(pl.multiple_of(z * groups, groups), groups), :], filter_ref),
            (skip_hbm.at[:, pl.ds(begin, own)], skip_ref),
        ))
    ]
    for load in loads:
        load.start()
    barrier = pltpu.get_barrier_semaphore()
    for peer in peers + [beside_y]:
        pl.semaphore_signal(barrier, inc=1, device_id=peer, device_id_type=MESH)

    def x_place(part, at):
        return x_all.at[pl.ds(2 * part, 2), pl.ds(pl.multiple_of(at * rows, rows), rows), :]

    x_targets = [((z + 1) * 2 + y, fsdp), ((z - 1) * 2 + y, fsdp), beside_x, beside_core]
    part_x = (1 - x) * 2 + core

    def x_copy(kind, part, at):
        block = part * line + at
        place = x_place(part, at)
        return remote(place, place, x_send.at[kind, block], x_recv.at[block], x_targets[kind])

    def x_arrive(part, at):
        place = x_place(part, at)
        block = part * line + at
        remote(place, place, x_send.at[0, block], x_recv.at[block], here).wait_recv()

    def x_pass(at, up, down):
        if up:
            visit_when(z < last, lambda: x_copy(0, fsdp, at).start())
        if down:
            visit_when(z > 0, lambda: x_copy(1, fsdp, at).start())
        x_copy(2, fsdp, at).start()
        x_copy(3, fsdp, at).start()

    def x_step(away):
        @pl.when(z >= away)
        def _():
            x_arrive(fsdp, z - away)
            x_pass(z - away, True, False)

        @pl.when(z + away <= last)
        def _():
            x_arrive(fsdp, z + away)
            x_pass(z + away, False, True)

    def x_over(away):
        def take(at):
            x_arrive(part_x, at)
            x_copy(3, part_x, at).start()

        if away == 0:
            take(z)
        else:
            visit_when(z >= away, lambda: take(z - away))
            visit_when(z + away <= last, lambda: take(z + away))

    cuts = [(kind, 1) for kind in range(kinds)]

    def piece(strip, cut, at):
        lanes = pl.ds(pl.multiple_of(at * own + strip * LANE, LANE), LANE)
        return weight_ref.at[cut[0], :, lanes]

    def landing(strip, cut, at, side):
        lanes = pl.ds(cut[0] * LANE, cut[1] * LANE)
        return w_all.at[2 * at + side, strip, :, lanes]

    def w_copy(strip, cut, to):
        return remote(
            piece(strip, cut, to), landing(strip, cut, z, y),
            w_send.at[to, strip, cut[0]], w_recv.at[2 * z + y, strip, cut[0]], level(to),
        )

    def w_over(strip, cut, at, mine):
        source = piece(strip, cut, z) if mine else landing(strip, cut, at, y)
        return remote(
            source, landing(strip, cut, at, y),
            y_send.at[at, strip, cut[0]], w_recv.at[2 * at + y, strip, cut[0]], beside_y,
        )

    def w_arrive(strip, cut, at, side):
        place = landing(strip, cut, at, side)
        remote(
            place, place, y_send.at[at, strip, cut[0]], w_recv.at[2 * at + side, strip, cut[0]], here
        ).wait_recv()

    others = [z + 1 - 2 * (z % 2), (z + 2) % line, last - z]

    def w_queue(goals):
        return [
            (strip, cut, goals[away]) for away, strip in SEND_ORDER[len(goals)] for cut in cuts
        ]

    def w_send_all(queue):
        for strip, cut, goal in queue:
            w_copy(strip, cut, goal).start()

    def w_early():
        for away in range(last):
            for at, goals in (
                (away, range(away + 1, line)), (last - away, range(last - away - 1, -1, -1))
            ):
                queue = w_queue(goals)[: SEND_EARLY[len(goals)]]
                if queue:
                    visit_when(z == at, functools.partial(w_send_all, queue))

    def w_rest(goals):
        w_send_all(w_queue(goals)[SEND_EARLY[len(goals)] :])

    def w_spread(away):
        above = range(away + 1, line)
        below = range(last - away - 1, -1, -1)
        if above:
            visit_when(z == away, lambda: w_rest(above))
            visit_when(z == last - away, lambda: w_rest(below))

    def w_turn(step, strip):
        for cut in cuts:
            w_arrive(strip, cut, others[step], y)
            w_over(strip, cut, others[step], False).start()

    def multiply(strip, at, side, cut, first=False):
        index = 2 * at + side

        def body(step, carry):
            span = pl.ds(pl.multiple_of(step * TILE, TILE), TILE)
            left = x_all[index, span, :]
            lanes = slice(cut[0] * LANE, (cut[0] + cut[1]) * LANE)
            part = jnp.dot(left, w_all[index, strip, :, lanes], preferred_element_type=jnp.float32)
            if first:
                acc[strip, span, lanes] = part
            else:
                acc[strip, span, lanes] += part
            return carry

        lax.fori_loop(0, rows * line // TILE, body, 0)

    def take(strip, at):
        for cut in cuts:
            w_arrive(strip, cut, at, 1 - y)
        multiply(strip, at, 1 - y, whole)

    s_targets = [beside_x, beside_core, (ctx, (1 - x) * 2 + 1 - core)]

    def s_copy(index):
        place = sums.at[fsdp]
        return remote(place, place, s_send.at[index], s_recv.at[fsdp], s_targets[index])

    def s_arrive(index):
        part = s_targets[index][1]
        place = sums.at[part]
        remote(place, place, s_send.at[index], s_recv.at[part], here).wait_recv()

    span = share // 4

    def o_over(index):
        rows_of = pl.ds(index * span, span)
        return remote(
            out_weight_ref.at[rows_of, :], o_all.at[core, y, rows_of],
            o_send.at[index], o_recv.at[index], beside_y,
        )

    def o_over_arrive(index):
        place = o_all.at[core, 1 - y, pl.ds(index * span, span)]
        remote(place, place, o_send.at[index], o_recv.at[index], here).wait_recv()

    def o_copy(side, own_half):
        place = o_all.at[core, side]
        slot = 4 if own_half else 5
        return remote(
            out_weight_ref if own_half else place, place,
            o_send.at[slot], o_recv.at[slot], beside_core,
        )

    def o_arrive(side, own_half):
        place = o_all.at[1 - core, side]
        slot = 4 if own_half else 5
        remote(place, place, o_send.at[slot], o_recv.at[slot], here).wait_recv()

    whole = (0, kinds)
    w_own = [
        pltpu.make_async_copy(
            piece(strip, cut, z), landing(strip, cut, z, y), w_local.at[strip, cut[0]]
        )
        for strip in range(strips) for cut in cuts
    ]
    o_own = pltpu.make_async_copy(out_weight_ref, o_all.at[core, y], o_local.at[0])

    loads[0].wait()
    values = tokens_ref[...].astype(jnp.float32)
    squares = values * values
    coarse = squares.astype(jnp.bfloat16)
    fine = (squares - coarse.astype(jnp.float32)).astype(jnp.bfloat16)
    ones = jnp.ones((8, features), jnp.bfloat16)
    contract = (((1,), (1,)), ((), ()))
    total = lax.dot_general(ones, coarse, contract, preferred_element_type=jnp.float32)
    total += lax.dot_general(ones, fine, contract, preferred_element_type=jnp.float32)
    sums[fsdp] = total
    pl.semaphore_wait(barrier, len(peers) + 1)
    for index in range(3):
        s_copy(index).start()
    w_early()
    for strip in range(strips):
        for cut in cuts:
            w_over(strip, cut, z, True).start()
    for copy in w_own:
        copy.start()
    o_own.start()
    o_copy(y, True).start()
    for load in loads[1:]:
        load.wait()
    for index in range(3):
        s_arrive(index)
    square = sums[0]
    for part in range(1, parts):
        square = square + sums[part]
    mean = square[:1] / (features * parts)
    scale = jnp.broadcast_to(lax.rsqrt(mean + 1e-06), (LANE, rows)).T
    scale = jnp.concatenate([scale] * (features // LANE), axis=1)
    normed = (values * scale * gain_ref[...]).astype(jnp.bfloat16)
    for side in range(2):
        x_all[2 * fsdp + side, pl.ds(pl.multiple_of(z * rows, rows), rows), :] = (
            normed[:, side * depth : (side + 1) * depth]
        )
    x_pass(z, True, True)
    w_spread(0)

    flip = (
        lax.broadcasted_iota(jnp.int32, (flen, flen), 0)
        + lax.broadcasted_iota(jnp.int32, (flen, flen), 1)
    ) == flen - 1
    turned = jnp.dot(filter_ref[...], flip.astype(jnp.bfloat16), preferred_element_type=jnp.float32)
    base = jnp.concatenate([turned, jnp.zeros_like(turned)], axis=1)
    base = pltpu.roll(base, 1, 1)
    for group in range(groups):
        row = jnp.broadcast_to(base[group : group + 1, :], (flen, 2 * flen))
        band = pltpu.roll(row, 0, 1, stride=1, stride_axis=0)
        bands[pl.ds(group * flen, flen), :] = band.astype(jnp.bfloat16)
    for strip in range(strips):
        halo_in[strip, 0] = jnp.zeros(halo_in.shape[2:], halo_in.dtype)

    def h_copy(slab, strip):
        return remote(
            halo_out.at[strip, slab], halo_in.at[strip, slab + 1],
            h_send.at[strip, slab], h_recv.at[strip, slab + 1], beside_y,
        )

    def h_arrive(slot, strip):
        place = halo_in.at[strip, slot]
        remote(place, place, h_send.at[strip, 0], h_recv.at[strip, slot], here).wait_recv()

    def tap(index, kind, strip):
        return taps_ref[index, kind : kind + 1, strip * LANE : (strip + 1) * LANE]

    every = range(kinds)

    def part_lanes(kind):
        return slice(kind * LANE, (kind + 1) * LANE)

    def edges(strip):
        for slab in range(line):
            start, end = slab * rows, (slab + 1) * rows
            for kind in every:
                exact = acc[strip, start:end, part_lanes(kind)].astype(jnp.bfloat16)
                acc[strip, start:end, part_lanes(kind)] = exact.astype(jnp.float32)
                halo_out[strip, slab, kind * 16 : (kind + 1) * 16, :] = exact[rows - 16 :]
            tails = []
            for kind in (1, 2):
                tails.append(
                    tap(0, kind, strip) * acc[strip, end - flen : end, part_lanes(kind)]
                    + tap(1, kind, strip) * acc[strip, end - flen - 1 : end - 1, part_lanes(kind)]
                    + tap(2, kind, strip) * acc[strip, end - flen - 2 : end - 2, part_lanes(kind)]
                )
            halo_out[strip, slab, kinds * 16 :, :] = (tails[0] * tails[1]).astype(jnp.bfloat16)
            h_copy(slab, strip).start()

    lane_group = lax.broadcasted_iota(jnp.int32, (flen, LANE), 1) // group_width

    def mix(slab, strip):
        if slab > 0:
            visit_when(y == 0, lambda: h_arrive(slab, strip))
        visit_when(y == 1, lambda: h_arrive(slab + 1, strip))
        start = slab * rows
        filtered = []
        for kind in every:
            ahead = halo_in[strip, slab + y, kind * 16 : (kind + 1) * 16, :].astype(jnp.float32)
            extended = jnp.concatenate([ahead[8:], acc[strip, start : start + rows, part_lanes(kind)]], axis=0)
            filtered.append(
                short_conv([tap(index, kind, strip) for index in range(3)], extended[6:])
            )
        gate, key_part, value_part = filtered
        product = (key_part * value_part).astype(jnp.bfloat16)
        reach = jnp.concatenate([halo_in[strip, slab + y, kinds * 16 :, :], product], axis=0)
        skip = skip_ref[:, strip * LANE : (strip + 1) * LANE]
        matrix = bands[strip * fold * flen : (strip + 1) * fold * flen, :]
        for at in range(0, rows, flen):
            spread = jnp.dot(
                matrix, reach[at : at + 2 * flen], preferred_element_type=jnp.float32
            )
            conv = spread[:flen]
            for group in range(1, fold):
                conv = jnp.where(
                    lane_group == group, spread[group * flen : (group + 1) * flen], conv
                )
            result = gate[at : at + flen] * (
                conv + skip * product[at : at + flen].astype(jnp.float32)
            )
            gated[
                start + at : start + at + flen,
                pl.ds(pl.multiple_of(z * own + strip * LANE, LANE), LANE),
            ] = result.astype(jnp.bfloat16)

    g_cuts = [(0, slab, 2) for slab in range(0, line, 2)] + [(1, slab, 1) for slab in range(line)]

    def g_place(index, at):
        strip, slab, count = g_cuts[index]
        lanes = pl.ds(pl.multiple_of(at * own + strip * LANE, LANE), LANE)
        return gated.at[pl.ds(slab * rows, count * rows), lanes]

    def g_copy(kind, index, at):
        place = g_place(index, at)
        return remote(
            place, place, g_send.at[kind, index, at], g_recv.at[index, at], x_targets[kind]
        )

    def g_arrive(index, at):
        place = g_place(index, at)
        remote(place, place, g_send.at[0, index, at], g_recv.at[index, at], here).wait_recv()

    def g_step(index, away):
        if away == 0:
            visit_when(z < last, lambda: g_copy(0, index, z).start())
            visit_when(z > 0, lambda: g_copy(1, index, z).start())
            return

        @pl.when(z >= away)
        def _():
            g_arrive(index, z - away)
            visit_when(z < last, lambda: g_copy(0, index, z - away).start())

        @pl.when(z + away <= last)
        def _():
            g_arrive(index, z + away)
            visit_when(z > 0, lambda: g_copy(1, index, z + away).start())

    def c_copy(slab):
        return remote(
            gated.at[pl.ds(pl.multiple_of(slab * rows + (1 - core) * half, half), half), :],
            gated_other.at[pl.ds(slab * half, half), :],
            c_send.at[slab], c_recv.at[slab], beside_core,
        )

    def t_copy(slab, side):
        return remote(
            cross_out.at[slab, side], cross_in.at[slab, side],
            t_send.at[slab, side], t_recv.at[slab, side], beside_x,
        )

    def project(slab):
        c_copy(slab).wait_recv()
        mine = gated[pl.ds(pl.multiple_of(slab * rows + core * half, half), half), :]
        other = gated_other[pl.ds(slab * half, half), :]
        for side in range(2):
            part = jnp.dot(mine, o_all[core, side], preferred_element_type=jnp.float32)
            part += jnp.dot(other, o_all[1 - core, side], preferred_element_type=jnp.float32)
            terms[side] = part
            kept[slab, side] = terms[side, pl.ds(pl.multiple_of(x * quarter, quarter), quarter), :]
            cross_out[slab, side] = terms[
                side, pl.ds(pl.multiple_of((1 - x) * quarter, quarter), quarter), :
            ].astype(jnp.bfloat16)
            t_copy(slab, side).start()

    def out_place(x_from, core_from, side):
        start = pl.multiple_of(core_from * half + x_from * quarter, quarter)
        width = out_weight_ref.shape[1]
        return out_ref.at[pl.ds(start, quarter), pl.ds(side * width, width)]

    lands = fsdp == z

    def f_copy(slab, side):
        return remote(
            ready.at[slab, side], out_place(x, core, side),
            f_send.at[slab, side], f_recv.at[fsdp, side], (slab * 2 + y, z),
        )

    def f_stay(slab, side):
        return pltpu.make_async_copy(
            ready.at[slab, side], out_place(x, core, side), f_local.at[side]
        )

    def hand_over(slab):
        stays = lands & (z == slab)
        for side in range(2):
            t_copy(slab, side).wait_recv()
            ready[slab, side] = (
                kept[slab, side] + cross_in[slab, side].astype(jnp.float32)
            ).astype(jnp.bfloat16)
            visit_when(stays, lambda: f_stay(slab, side).start())
            visit_when(jnp.logical_not(stays), lambda: f_copy(slab, side).start())

    edge = (z == 0) | (z == last)
    first_pieces = range(line // 2)

    def stop(index):
        def turns(plan):
            for step, strip in plan.get(index, ()):
                w_turn(step, strip)

        visit_when(edge, lambda: turns(EDGE_TURNS))
        visit_when(jnp.logical_not(edge), lambda: turns(INNER_TURNS))
        for part in OUT_STOPS.get(index, ()):
            o_over(part).start()

    x_step(1)
    w_spread(1)
    stop(0)
    x_step(2)
    w_spread(2)
    x_over(0)
    stop(1)
    x_step(3)
    stop(2)
    x_over(1)
    x_over(2)
    stop(3)
    x_over(3)
    for part in (x * 2 + 1 - core, (1 - x) * 2 + 1 - core):
        for at in range(line):
            x_arrive(part, at)
    for copy in w_own:
        copy.wait()
    for strip in range(strips):
        multiply(strip, z, y, whole, True)
        take(strip, z)
    stop(4)
    multiply(0, others[0], y, whole)
    stop(5)
    multiply(0, others[2], y, whole)
    multiply(0, others[1], y, whole)
    stop(6)
    for step in (0, 2, 1):
        take(0, others[step])
    stop(7)
    edges(0)
    stop(8)
    for slab in range(line):
        mix(slab, 0)
        if slab % 2:
            g_step(slab // 2, 0)
    stop(9)
    for step in (0, 2, 1):
        multiply(1, others[step], y, whole)
    take(1, others[0])
    for index in first_pieces:
        g_step(index, 1)
    take(1, others[2])
    take(1, others[1])
    edges(1)
    stop(10)
    for index in first_pieces:
        g_step(index, 2)

    def slab_at(turn):
        return SLAB_ORDER[turn] if 0 <= turn < line else None

    for turn in range(line + 5):
        if turn < line:
            mix(slab_at(turn), 1)
            g_step(line // 2 + slab_at(turn), 0)
        if turn == 1:
            for index in first_pieces:
                g_step(index, 3)
        for away in range(1, line):
            slab = slab_at(turn - away)
            if slab is not None:
                g_step(line // 2 + slab, away)
        slab = slab_at(turn - last)
        if slab is not None:
            c_copy(slab).start()
        if turn == line - 1:
            for part in range(4):
                o_over_arrive(part)
            o_copy(1 - y, False).start()
            o_own.wait()
            o_arrive(y, True)
            o_arrive(1 - y, False)
        slab = slab_at(turn - last - 1)
        if slab is not None:
            project(slab)
        slab = slab_at(turn - last - 2)
        if slab is not None:
            hand_over(slab)

    for source in range(parts):
        @pl.when(jnp.logical_not(lands & (fsdp == source)))
        def _():
            for side in range(2):
                place = out_place(source // 2, source % 2, side)
                remote(
                    ready.at[0, side], place, f_send.at[0, side], f_recv.at[source, side], here
                ).wait_recv()

    for at in range(line):
        visit_when((z >= at) & (z < last), lambda: x_copy(0, fsdp, at).wait_send())
        visit_when((z <= at) & (z > 0), lambda: x_copy(1, fsdp, at).wait_send())
        x_copy(2, fsdp, at).wait_send()
        x_copy(3, fsdp, at).wait_send()
        x_copy(3, part_x, at).wait_send()
        for strip in range(strips):
            for cut in cuts:
                w_over(strip, cut, at, False).wait_send()
    for index in range(3):
        s_copy(index).wait_send()
    for strip in range(strips):
        for cut in cuts:
            for step in range(3):
                w_copy(strip, cut, others[step]).wait_send()
        visit_when(y == 0, lambda: h_arrive(line, strip))
        for slab in range(line):
            h_copy(slab, strip).wait_send()
    for part in range(4):
        o_over(part).wait_send()
    o_copy(y, True).wait_send()
    o_copy(1 - y, False).wait_send()
    for index in range(len(g_cuts)):
        for at in range(line):
            visit_when((z >= at) & (z < last), lambda: g_copy(0, index, at).wait_send())
            visit_when((z <= at) & (z > 0), lambda: g_copy(1, index, at).wait_send())
    for slab in range(line):
        c_copy(slab).wait_send()
        for side in range(2):
            t_copy(slab, side).wait_send()
        stays = lands & (z == slab)
        for side in range(2):
            visit_when(stays, lambda: f_stay(slab, side).wait())
            visit_when(jnp.logical_not(stays), lambda: f_copy(slab, side).wait_send())


ANY_SPEC = pl.BlockSpec(memory_space=pl.ANY)
DMA = pltpu.SemaphoreType.DMA


def level_plan(tokens, norm_gain, in_weight, short_filter, long_filter, skip_gain, out_weight):
    slabs, parts = lax.axis_size("ctx"), lax.axis_size("fsdp")
    line = slabs // 2
    rows, features = tokens.shape
    depth, kinds, share = in_weight.shape
    own = share // line
    flen = long_filter.shape[1]
    group_width = share // long_filter.shape[0]
    groups = own // group_width
    strips = own // LANE
    pieces = line // 2 + line
    positions = rows * line
    columns = out_weight.shape[1]
    low, full = jnp.bfloat16, jnp.float32
    half, quarter = rows // 2, rows // 4
    return pl.pallas_call(
        functools.partial(block_kernel, group_width),
        out_shape=jax.ShapeDtypeStruct(tokens.shape, low),
        in_specs=[ANY_SPEC] * 7,
        out_specs=ANY_SPEC,
        scratch_shapes=[
            pltpu.VMEM(tokens.shape, low),
            pltpu.VMEM((1, features), full),
            pltpu.VMEM((3, kinds, own), full),
            pltpu.VMEM((groups, flen), low),
            pltpu.VMEM((1, own), full),
            pltpu.VMEM((2 * parts, positions, depth), low),
            pltpu.VMEM((slabs, strips, depth, kinds * LANE), low),
            pltpu.VMEM((strips, positions, kinds * LANE), full),
            pltpu.VMEM((parts, 8, rows), full),
            pltpu.VMEM((groups * flen, 2 * flen), low),
            pltpu.VMEM((strips, line, kinds * 16 + flen, LANE), low),
            pltpu.VMEM((strips, line + 1, kinds * 16 + flen, LANE), low),
            pltpu.VMEM((positions, share), low),
            pltpu.VMEM((positions // 2, share), low),
            pltpu.VMEM((2, 2, share, columns), low),
            pltpu.VMEM((2, half, columns), full),
            pltpu.VMEM((line, 2, quarter, columns), full),
            pltpu.VMEM((line, 2, quarter, columns), low),
            pltpu.VMEM((line, 2, quarter, columns), low),
            pltpu.VMEM((line, 2, quarter, columns), low),
            DMA((5,)), DMA((4, parts * line)), DMA((parts * line,)),
            DMA((3,)), DMA((parts,)),
            DMA((strips, kinds)), DMA((line, strips, kinds)), DMA((line, strips, kinds)),
            DMA((slabs, strips, kinds)),
            DMA((strips, line)), DMA((strips, line + 1)),
            DMA((2, pieces, line)), DMA((pieces, line)),
            DMA((line,)), DMA((line,)),
            DMA((1,)), DMA((6,)), DMA((6,)),
            DMA((line, 2)), DMA((line, 2)),
            DMA((2,)), DMA((line, 2)), DMA((parts, 2)),
        ],
        compiler_params=pltpu.CompilerParams(
            collective_id=0, has_side_effects=True, vmem_limit_bytes=63 * 2**20
        ),
    )(
        tokens, norm_gain[None], in_weight.transpose(1, 0, 2), short_filter,
        long_filter, skip_gain[None], out_weight,
    )


def on_device(tokens, *rest):
    slabs, parts = lax.axis_size("ctx"), lax.axis_size("fsdp")
    depth, _, share = rest[1].shape
    groups, flen = rest[3].shape
    own = share // (slabs // 2)
    fits = (
        parts == 4 and slabs == 8 and tokens.shape[0] == 2 * flen and flen == LANE
        and tokens.shape[1] == 2 * depth and own == 2 * LANE and 2 * rest[5].shape[1] == share and share == tokens.shape[1]
        and LANE % (share // groups) == 0 and depth * share <= 2**19
    )
    return (level_plan if fits else slab_plan)(tokens, *rest)


def solution(mesh):
    in_specs = (
        P("ctx", "fsdp"),
        P(),
        P("ctx", None, "fsdp"),
        P(None, None, "fsdp"),
        P("fsdp", None),
        P("fsdp"),
        P("fsdp", "ctx"),
    )
    out_specs = P("ctx", "fsdp")
    return jax.shard_map(
        on_device, mesh=mesh, in_specs=in_specs, out_specs=out_specs, check_vma=False
    )
```
